32 devices in a mesh: row: 4 (over z), col: 4 (over y, x), feat: 2 (over core).
Axes of the slice: x: 2, y: 2, z: 4, core: 2. Of those that a mesh axis runs over, the one named last changes fastest.
Arguments:
- tile_values: bfloat16 [4, 4, 80, 128, 128], P('row', 'col')
- tile_rows: int32 [4, 4, 80], P('row', 'col'), may hold values from 0 to 15, as said below
- tile_cols: int32 [4, 4, 80], P('row', 'col'), may hold values from 0 to 15
- tile_mask: int32 [4, 4, 80], P('row', 'col'), may hold values from 0 to 1, as said below
- degree_caps: int32 [8192], P(('row', 'col')), may hold values from 1 to 32, as said below
- clip_groups: int32 [8192], P(('row', 'col')), may hold values from 0 to 7
- clip_bounds: float32 [8], replicated, may hold values from 51.2 to 256
- features: bfloat16 [8192, 256], P('col', 'feat')
- weight: bfloat16 [256, 256], replicated, may hold values from -0.375 to 0.375
- out_grad: bfloat16 [8192, 256], P(('row', 'col'), 'feat')
- dp_noise: float32 [256, 256], P(None, 'feat'), may hold values from -6 to 6
Outputs:
- out_feat: bfloat16 [8192, 256], P(('row', 'col'), 'feat')
- grad_weight: float32 [256, 256], P(None, 'feat')
- grad_input: bfloat16 [8192, 256], P('col', 'feat')
The draws below stay inside these ranges and needn't reach their ends.
Inputs may be any that keep to these rules, and one draw needn't show every extreme that they name: `tile_rows`: each tile slot of one pair of row and col indices names a distinct pair of block row and block column. `tile_mask`: at most all 80 slots of one pair of row and col indices are live; in every draw some pair has all of them live. degree_caps[i] is the number of nonzero entries in row i of A, raised to 1 where it is 0 and capped at 32.
All inputs are finite; a program needn't handle non-finite values.
Results may differ from the reference program's by a relative error of at most 0.006.
Values may be sent and summed in bfloat16 or wider, within the bound.
A program may use at most 128 MiB of HBM per device.

```python
import math
import jax
import jax.numpy as jnp
from jax import lax

BLK = 128
HID = 256
NODE_DEV = 512
TILE_ROW = 5
GROUPS = 8
NODES = 8192
RBLK = 16
CBLK = 16
TPD = 80
N_ROW = 4
N_COL = 4


def tile_layout(key):
    key = jax.random.fold_in(key, 7)
    key_score, key_shuffle, key_rank, key_light = jax.random.split(key, 4)
    pairs = RBLK * CBLK
    slot_total = TPD
    pair_ids = jnp.arange(pairs, dtype=jnp.int32)
    pair_row = pair_ids // CBLK
    pair_col = pair_ids % CBLK
    dev_row = jnp.arange(N_ROW, dtype=jnp.int32)[:, None, None]
    dev_col = jnp.arange(N_COL, dtype=jnp.int32)[None, :, None]
    distance = jnp.abs(dev_row * RBLK + pair_row - dev_col * CBLK - pair_col)
    score = jax.random.randint(key_score, (N_ROW, N_COL, pairs), 0, 2 * CBLK) + jnp.minimum(distance, 2 * CBLK)
    unique = score * pairs + pair_ids
    _, picked = lax.top_k(-unique, slot_total)
    slot_ids = jnp.arange(slot_total, dtype=jnp.int32)
    shuffle_keys = jax.random.randint(key_shuffle, (N_ROW, N_COL, slot_total), 0, 1 << 20) * slot_total + slot_ids
    shuffle = jnp.argsort(shuffle_keys, axis=-1, stable=True)
    picked = jnp.take_along_axis(picked, shuffle, axis=-1)
    rank_keys = jax.random.randint(key_rank, (N_ROW, N_COL, slot_total), 0, 1 << 20) * slot_total + slot_ids
    rank = jnp.argsort(jnp.argsort(rank_keys, axis=-1, stable=True), axis=-1, stable=True)
    heavy = (dev_row * RBLK < (dev_col + 1) * CBLK) & (dev_col * CBLK < (dev_row + 1) * RBLK)
    light = jax.random.randint(key_light, (N_ROW, N_COL, 1), slot_total // 5, slot_total // 2 + 1)
    live_count = jnp.where(heavy, slot_total, light)
    mask_out = (rank < live_count).astype(jnp.int32)
    return ((picked // CBLK).astype(jnp.int32), (picked % CBLK).astype(jnp.int32), mask_out)


def tile_keep(key):
    key_keep = jax.random.fold_in(key, 11)
    rate = max(1, TILE_ROW * N_COL * BLK // 48)
    shape = (N_ROW, N_COL, TPD, BLK, BLK)
    return jax.random.randint(key_keep, shape, 0, rate) == 0


def draw_tile_rows(key, part):
    return tile_layout(key)[0]


def draw_tile_cols(key, part):
    return tile_layout(key)[1]


def draw_tile_mask(key, part):
    return tile_layout(key)[2]


def draw_tile_values(key, part):
    keep = tile_keep(key).astype(jnp.float32)
    key_value = jax.random.fold_in(key, 19)
    shape = (N_ROW, N_COL, TPD, BLK, BLK)
    values = jax.random.normal(key_value, shape, jnp.float32)
    return (values * keep * 0.25).astype(jnp.bfloat16)


def draw_degree_caps(key, part):
    rows_out, cols_out, mask_out = tile_layout(key)
    keep = tile_keep(key)
    row_count = jnp.sum(keep.astype(jnp.int32), axis=-1) * mask_out[..., None]
    dev_row = jnp.arange(N_ROW, dtype=jnp.int32)[:, None, None]
    global_block = dev_row * RBLK + rows_out
    node_ids = global_block[..., None] * BLK + jnp.arange(BLK, dtype=jnp.int32)[None, None, None, :]
    counts = jax.ops.segment_sum(row_count.reshape(-1), node_ids.reshape(-1), num_segments=NODES)
    return jnp.clip(counts, 1, 32).astype(jnp.int32)


def draw_features(key, part):
    key_col, key_value = jax.random.split(jax.random.fold_in(key, 13))
    col_scale = jnp.exp(jax.random.uniform(key_col, (HID,), jnp.float32) * math.log(10.0))
    values = jax.random.normal(key_value, (NODES, HID), jnp.float32)
    return (values * col_scale[None, :] * 0.4).astype(jnp.bfloat16)


def draw_out_grad(key, part):
    key_row, key_col, key_value = jax.random.split(jax.random.fold_in(key, 17), 3)
    row_scale = jnp.exp(jax.random.uniform(key_row, (NODES,), jnp.float32) * math.log(10.0))
    col_scale = jnp.exp(jax.random.uniform(key_col, (HID,), jnp.float32) * math.log(10.0))
    values = jax.random.normal(key_value, (NODES, HID), jnp.float32)
    return (values * row_scale[:, None] * col_scale[None, :] * 0.3).astype(jnp.bfloat16)


def touch_ends(values, key, smallest, top_value):
    longest = values.shape.index(max(values.shape))
    spots = []
    for shift in (0, 1):
        where = [jax.random.randint(jax.random.fold_in(key, axis), (), 0, length) for axis, length in enumerate(values.shape)]
        where[longest] = (where[longest] + shift) % values.shape[longest]
        spots.append(tuple(where))
    return values.at[spots[0]].set(smallest).at[spots[1]].set(top_value)


def shard_levels(key, shape, pieces, least, top_value):
    def one(dim, shards_of):
        draws = jax.random.uniform(jax.random.fold_in(jax.random.fold_in(key, 6), dim), (shards_of,), jnp.float32, least / len(pieces), top_value / len(pieces))
        return jnp.repeat(jnp.exp(draws), shape[dim] // shards_of).reshape((-1,) + (1,) * (len(shape) - dim - 1))

    level = one(*pieces[0])
    for cut in pieces[1:]:
        level = level * one(*cut)
    return level


def noise(stream_key, dims, deviation, bound, shards=(), kind=jnp.bfloat16):
    result = jax.random.normal(stream_key, dims, jnp.float32) * deviation
    if len(shards) > 0:
        result = shard_levels(stream_key, dims, shards, -0.22, 0.18) * result
    return jnp.clip(result, min=-bound, max=bound).astype(kind)


def setup_inputs(seed: int = 0) -> dict:
    key_of = jax.random.split(jax.random.key(seed), 12)
    return {
        "tile_values": draw_tile_values(jax.random.fold_in(key_of[11], 71), 0),
        "tile_rows": draw_tile_rows(jax.random.fold_in(key_of[11], 71), 0),
        "tile_cols": draw_tile_cols(jax.random.fold_in(key_of[11], 71), 0),
        "tile_mask": draw_tile_mask(jax.random.fold_in(key_of[11], 71), 0),
        "degree_caps": draw_degree_caps(jax.random.fold_in(key_of[11], 71), 0),
        "clip_groups": touch_ends(jax.random.randint(key_of[5], (NODES,), 0, GROUPS), jax.random.fold_in(key_of[5], 1), 0, GROUPS - 1).astype(jnp.int32),
        "clip_bounds": jnp.clip(jnp.exp(jax.random.uniform(key_of[6], (GROUPS,), jnp.float32, math.log(51.2), math.log(256.0))), 51.2, 256.0),
        "features": draw_features(jax.random.fold_in(key_of[11], 71), 0),
        "weight": noise(key_of[8], (HID, HID), HID ** -0.5, 0.375),
        "out_grad": draw_out_grad(jax.random.fold_in(key_of[11], 71), 0),
        "dp_noise": noise(key_of[10], (HID, HID), 1.0, 6.0, ((1, 2),), jnp.float32),
    }


def reference(tile_values, tile_rows, tile_cols, tile_mask, degree_caps, clip_groups, clip_bounds, features, weight, out_grad, dp_noise):
    row_span = NODE_DEV * N_COL
    col_span = NODE_DEV * N_ROW
    width = features.shape[1]
    feat_full = features.astype(jnp.float32)
    device_ids = jnp.arange(N_ROW * N_COL, dtype=jnp.int32)

    def forward_step(totals, device):
        row_idx = device // N_COL
        col_idx = device % N_COL
        tile_vals = tile_values[row_idx, col_idx].astype(jnp.float32)
        source = lax.dynamic_slice_in_dim(feat_full, (col_idx * col_span).astype(jnp.int32), col_span, 0)
        source = source.reshape(CBLK, BLK, width)
        picked = source[tile_cols[row_idx, col_idx]]
        products = jnp.einsum('kij,kjf->kif', tile_vals, picked)
        target = jnp.where(tile_mask[row_idx, col_idx] == 1, tile_rows[row_idx, col_idx], RBLK)
        part_sum = jax.ops.segment_sum(products, target, num_segments=RBLK + 1)[:RBLK].reshape(row_span, width)
        start = (row_idx * row_span).astype(jnp.int32)
        old_sum = lax.dynamic_slice_in_dim(totals, start, row_span, 0)
        return (lax.dynamic_update_slice_in_dim(totals, old_sum + part_sum, start, 0), None)
    raw_sum, _ = lax.scan(forward_step, jnp.zeros((NODES, width), jnp.float32), device_ids)
    node_scale = lax.rsqrt(degree_caps.astype(jnp.float32))[:, None]
    aggregate = (raw_sum * node_scale).astype(jnp.bfloat16)
    pre_act = jnp.dot(aggregate, weight, preferred_element_type=jnp.float32)
    out_feat = jax.nn.silu(pre_act).astype(jnp.bfloat16)
    gate_sig = jax.nn.sigmoid(pre_act)
    grad_pre = (out_grad.astype(jnp.float32) * gate_sig * (1.0 + pre_act * (1.0 - gate_sig))).astype(jnp.bfloat16)
    agg_sq = lax.optimization_barrier(jnp.sum(jnp.square(aggregate.astype(jnp.float32)), axis=1))
    grad_sq = lax.optimization_barrier(jnp.sum(jnp.square(grad_pre.astype(jnp.float32)), axis=1))
    bounds = clip_bounds[clip_groups]
    factor = jnp.minimum(1.0, bounds / (jnp.sqrt(agg_sq + 1e-06) * jnp.sqrt(grad_sq + 1e-06)))
    clipped = (factor[:, None] * grad_pre.astype(jnp.float32)).astype(jnp.bfloat16)
    total_grad = jnp.dot(aggregate.T, clipped, preferred_element_type=jnp.float32)
    grad_weight = total_grad * (1.0 / math.sqrt(NODES)) + dp_noise
    back_prod = jnp.dot(grad_pre, weight.T, preferred_element_type=jnp.float32)
    grad_agg = (back_prod * node_scale).astype(jnp.bfloat16)
    grad_full = grad_agg.astype(jnp.float32)

    def backward_step(totals, device):
        row_idx = device // N_COL
        col_idx = device % N_COL
        tile_vals = tile_values[row_idx, col_idx].astype(jnp.float32)
        source = lax.dynamic_slice_in_dim(grad_full, (row_idx * row_span).astype(jnp.int32), row_span, 0)
        source = source.reshape(RBLK, BLK, width)
        picked = source[tile_rows[row_idx, col_idx]]
        products = jnp.einsum('kji,kjf->kif', tile_vals, picked)
        target = jnp.where(tile_mask[row_idx, col_idx] == 1, tile_cols[row_idx, col_idx], CBLK)
        part_sum = jax.ops.segment_sum(products, target, num_segments=CBLK + 1)[:CBLK].reshape(col_span, width)
        start = (col_idx * col_span).astype(jnp.int32)
        old_sum = lax.dynamic_slice_in_dim(totals, start, col_span, 0)
        return (lax.dynamic_update_slice_in_dim(totals, old_sum + part_sum, start, 0), None)
    input_sum, _ = lax.scan(backward_step, jnp.zeros((NODES, width), jnp.float32), device_ids)
    grad_input = input_sum.astype(jnp.bfloat16)
    return (out_feat, grad_weight, grad_input)
```

```python
import functools
import math

import jax
import jax.numpy as jnp
from jax import lax
from jax.experimental import pallas as pl
from jax.experimental.pallas import tpu as pltpu
from jax.sharding import PartitionSpec as P

MESH = pl.DeviceIdType.MESH
LANES = 128
PIECE = 256
CHUNKS = 2
PARTS = 2
LOADS = 4
LAG = 5
LAG_STEP = 11


def layer(
    n_row, n_col, scale, cached,
    tiles_hbm, rows_hbm, cols_hbm, mask_hbm, caps_hbm, groups_hbm, bounds_hbm,
    feats_hbm, weight_hbm, og_hbm, noise_hbm,
    out_feat_hbm, grad_weight_hbm, grad_input_hbm,
    rows_s, cols_s, mask_s, bounds_s, map_s, map_v, caps, groups,
    feats, weight, out_grad, noise, out_feat, grad_weight, grad_input,
    tiles, dense, strip, rs_send, rs_recv, own_send, chip_part, og_peer,
    scale_col, bound_col, feat_halves, back_t, grads,
    w_send, w_recv, w_all, w_col, w_fin,
    z_send, z_out, z_in, z_fin,
    small_sem, map_sem, tile_sem, in_sem, out_sem, gin_sem, og_sem, own_sem, of_sem,
    rs_ssem, rs_rsem, ag_ssem, ag_rsem, own_ag_sem,
    wz_ssem, wz_rsem, wa_ssem, wa_rsem, wc_ssem, wc_rsem, wf_ssem, wf_rsem,
    z_ssem, z_fsem, zo_rsem, zi_rsem,
):
    row, col, feat = lax.axis_index("row"), lax.axis_index("col"), lax.axis_index("feat")
    other = 1 - feat
    f32, bf16 = jnp.float32, jnp.bfloat16
    slots, blk = tiles_hbm.shape[0], tiles_hbm.shape[1]
    node, half = og_hbm.shape
    col_range = feats.shape[0]
    col_blocks = col_range // blk
    sub = node // blk
    mine = node // 2
    nb = mine // PARTS
    hid = weight.shape[0]
    fc = half // CHUNKS
    pieces = col_range // PIECE
    side = math.isqrt(n_col)
    side = side if side * side == n_col else n_col
    col_x, col_y = lax.rem(col, side), lax.div(col, side)
    wr, wc = hid // n_row, hid // n_col

    def remote(src, dst, ssem, rsem, where):
        return pltpu.make_async_remote_copy(
            src_ref=src, dst_ref=dst, send_sem=ssem, recv_sem=rsem,
            device_id=where, device_id_type=MESH,
        )

    def peer_to(k):
        x, y = k % side, k // side
        return lax.rem(col_y + y, n_col // side) * side + lax.rem(col_x + x, side)

    def peer_from(k):
        x, y = k % side, k // side
        up = n_col // side
        return lax.rem(col_y - y + up, up) * side + lax.rem(col_x - x + side, side)

    small = [
        pltpu.make_async_copy(src, dst, small_sem.at[i])
        for i, (src, dst) in enumerate((
            (rows_hbm, rows_s), (cols_hbm, cols_s), (mask_hbm, mask_s), (bounds_hbm, bounds_s),
            (caps_hbm, caps), (groups_hbm, groups),
        ))
    ]
    count = slots // LOADS
    loads = [
        pltpu.make_async_copy(
            tiles_hbm.at[pl.ds(i * count, count)], tiles.at[pl.ds(i * count, count)], tile_sem.at[i]
        )
        for i in range(LOADS)
    ]
    inputs = [
        pltpu.make_async_copy(src, dst, in_sem.at[i])
        for i, (src, dst) in enumerate(
            ((feats_hbm, feats), (og_hbm, out_grad), (weight_hbm, weight), (noise_hbm, noise))
        )
    ]
    for copy in small + inputs[:1] + loads + inputs[1:]:
        copy.start()

    barrier = pltpu.get_barrier_semaphore()

    def greet(where):
        pl.semaphore_signal(barrier, inc=1, device_id=where, device_id_type=MESH)

    greet({"feat": other})
    for g in range(2):
        for k in range(1, n_col):
            greet({"col": peer_to(k), "feat": g})
        for step in range(1, n_row):
            greet({"row": lax.rem(row + step, n_row), "feat": g})

    tiles[slots] = jnp.zeros((blk, blk), bf16)
    for copy in small[:3]:
        copy.wait()
    spot = lax.broadcasted_iota(jnp.int32, map_v.shape, 0) * LANES + lax.broadcasted_iota(jnp.int32, map_v.shape, 1)

    def place(k, found):
        at = jnp.where(mask_s[k] == 1, rows_s[k] * col_blocks + cols_s[k], -1)
        return jnp.where(spot == at, k, found)

    map_v[...] = lax.fori_loop(0, slots, place, jnp.full(map_v.shape, slots, jnp.int32), unroll=8)
    map_copy = pltpu.make_async_copy(map_v, map_s, map_sem.at[0])
    map_copy.start()
    for copy in small[3:]:
        copy.wait()

    def column(values):
        return jnp.transpose(jnp.broadcast_to(values, (LANES, mine)))

    my_nodes = pl.ds(pl.multiple_of(feat * mine, mine), mine)
    scale_row = lax.rsqrt(caps[:, my_nodes].astype(f32))
    scale_col[...] = column(scale_row)
    bound = jnp.zeros((1, mine), f32)
    for g in range(bounds_s.shape[0]):
        bound = bound + jnp.where(groups[:, my_nodes] == g, bounds_s[g], 0.0)
    bound_col[...] = column(bound)
    map_copy.wait()
    inputs[0].wait()
    for copy in loads:
        copy.wait()

    def which(index):
        return map_s[index // LANES, index % LANES] if isinstance(index, int) else map_s[lax.div(index, LANES), lax.rem(index, LANES)]

    def assemble(chunk, h):
        base = chunk * node if cached else 0
        for g in range(2):
            for b in range(nb // blk):
                rb = (g * mine + h * nb) // blk + b
                at = pl.ds(pl.multiple_of(base + rb * blk, blk), blk)
                for cb in range(col_blocks):
                    tile = which((chunk * sub + rb) * col_blocks + cb)
                    dense[at, cb * blk:(cb + 1) * blk] = tiles[tile]

    def partial_sum(chunk, h):
        assemble(chunk, h)
        base = chunk * node if cached else 0
        left = jnp.concatenate(
            [dense[pl.ds(pl.multiple_of(base + g * mine + h * nb, blk), nb), :] for g in range(2)], axis=0
        )
        return jnp.dot(left, feats[...], preferred_element_type=f32)

    def rs_copy(k, h, g, sender):
        return remote(
            rs_send.at[k - 1, g, h], rs_recv.at[k - 1, sender, h],
            rs_ssem.at[k - 1, g, h], rs_rsem.at[k - 1, sender, h],
            {"col": peer_to(k), "feat": g},
        )

    def make(k, h):
        part = partial_sum(peer_to(k), h).astype(bf16)
        for g in range(2):
            rs_send[k - 1, g, h] = part[g * nb:(g + 1) * nb]

    def push(k, h):
        for g in range(2):
            rs_copy(k, h, g, feat).start()

    def own_copy(h, sender):
        return remote(
            own_send.at[1 - sender, h], chip_part.at[sender, h],
            own_sem.at[0, h], own_sem.at[1, h], {"feat": other},
        )

    def make_own(h):
        part = partial_sum(col, h)
        for g in range(2):
            own_send[g, h] = part[g * nb:(g + 1) * nb]
        own_copy(h, feat).start()
        chip_part[feat, h] = own_send[feat, h]

    make(n_col - 1, 0)
    pl.semaphore_wait(barrier, 2 * (n_col + n_row) - 3)
    push(n_col - 1, 0)
    for copy in inputs[1:]:
        copy.wait()
    theirs = pl.ds(pl.multiple_of(other * mine, mine), mine)
    og_copy = remote(out_grad.at[theirs], og_peer, og_sem.at[0], og_sem.at[1], {"feat": other})
    og_copy.start()

    for h in range(PARTS):
        def forward(i, carry):
            k = n_col - 1 - i
            make(k, h)
            push(k, h)
            return carry

        lax.fori_loop(1 if h == 0 else 0, n_col - 1, forward, 0)
        make_own(h)

    def block_of(c, g, h):
        return (c * 2 + g) * PARTS + h

    def ag_copy(ch, k, g, h, sender):
        return remote(
            back_t.at[g, ch, h], grads.at[ch, sender],
            ag_ssem.at[ch, k - 1, g, h], ag_rsem.at[ch, sender], {"col": peer_to(k), "feat": g},
        )

    def own_ag(ch, h, g, sender):
        return remote(
            back_t.at[g, ch, h], grads.at[ch, sender],
            own_ag_sem.at[ch, h], ag_rsem.at[ch, sender], {"feat": other},
        )

    w_total = jnp.zeros((hid, hid), f32)
    og_copy.wait()
    for h in range(PARTS):
        spot_h = slice(h * nb, (h + 1) * nb)
        own_copy(h, other).wait_recv()
        sums = [chip_part[0, h], chip_part[1, h]]
        for k in range(n_col - 1, 0, -1):
            for g in range(2):
                rs_copy(k, h, g, g).wait_recv()
                sums[g] = sums[g] + rs_recv[k - 1, g, h].astype(f32)
        node_scale = scale_col[spot_h]
        agg = jnp.concatenate([(s * node_scale).astype(bf16) for s in sums], axis=1)
        here = pl.ds(pl.multiple_of(feat * mine + h * nb, nb), nb)
        mine_og = out_grad[here]
        peer_og = og_peer[spot_h]
        cotangent = jnp.concatenate(
            [jnp.where(feat == 0, mine_og, peer_og), jnp.where(feat == 0, peer_og, mine_og)], axis=1
        )
        pre = jnp.dot(agg, weight[...], preferred_element_type=f32)
        sig = 1.0 / (1.0 + jnp.exp(-pre))
        grad = (cotangent.astype(f32) * sig * (1.0 + pre * (1.0 - sig))).astype(bf16)
        back = lax.dot_general(grad, weight[...], (((1,), (1,)), ((), ())), preferred_element_type=f32)
        back = (jnp.transpose(back) * scale_row[:, spot_h]).astype(bf16)
        for g in range(2):
            for ch in range(CHUNKS):
                at = g * half + ch * fc
                back_t[g, ch, h] = back[at:at + fc]
        me = block_of(col, feat, h)
        for ch in range(CHUNKS):
            for k in range(n_col - 1, 0, -1):
                for g in range(2):
                    ag_copy(ch, k, g, h, me).start()
            own_ag(ch, h, other, me).start()
            grads[ch, me] = back_t[feat, ch, h]
        activated = (pre * sig).astype(bf16)
        for g in range(2):
            feat_halves[g, h * nb:(h + 1) * nb] = activated[:, g * half:(g + 1) * half]

        def norm(value):
            value = value.astype(f32)
            return jnp.sqrt(jnp.sum(value * value, axis=1, keepdims=True) + 1e-06)

        factor = jnp.minimum(1.0, bound_col[spot_h] / (norm(agg) * norm(grad)))
        wide = grad.astype(f32)
        clipped = jnp.concatenate(
            [(factor * wide[:, g * half:(g + 1) * half]).astype(bf16) for g in range(2)], axis=1
        )
        w_total = w_total + lax.dot_general(agg, clipped, (((0,), (0,)), ((), ())), preferred_element_type=f32)

    def wz_copy(step, g, r, s):
        return remote(
            w_send.at[g, lax.rem(row + step, n_row)], w_recv.at[r, s],
            wz_ssem.at[step, g], wz_rsem.at[r, s], {"row": lax.rem(row + step, n_row), "feat": g},
        )

    def wz_own(r, s):
        return remote(
            w_send.at[other, row], w_recv.at[r, s], wz_ssem.at[0, 0], wz_rsem.at[r, s], {"feat": other}
        )

    for g in range(2):
        for r in range(n_row):
            w_send[g, r] = w_total[r * wr:(r + 1) * wr, g * half:(g + 1) * half].astype(bf16)
    w_recv[row, feat] = w_send[feat, row]
    for step in range(1, n_row):
        for g in range(2):
            wz_copy(step, g, row, feat).start()
    wz_own(row, feat).start()

    kept = pl.ds(pl.multiple_of(feat * mine, mine), mine)
    of_copy = remote(feat_halves.at[other], out_feat.at[kept], of_sem.at[0], of_sem.at[1], {"feat": other})
    of_copy.start()
    out_feat[kept] = feat_halves[feat]

    def w_rows(index, size):
        return pl.ds(pl.multiple_of(index * size, size), size)

    def wa_copy(step, sender):
        at = w_all.at[w_rows(sender, wr)]
        return remote(at, at, wa_ssem.at[step - 1], wa_rsem.at[sender], {"row": lax.rem(row + step, n_row)})

    def wc_copy(k, sender):
        return remote(
            w_all.at[w_rows(peer_to(k), wc)], w_col.at[sender], wc_ssem.at[k - 1], wc_rsem.at[sender],
            {"col": peer_to(k)},
        )

    def wf_copy(k, sender):
        at = w_fin.at[w_rows(sender, wc)]
        return remote(at, at, wf_ssem.at[k - 1], wf_rsem.at[sender], {"col": peer_to(k)})

    def weight_rows():
        for step in range(1, n_row):
            for g in range(2):
                wz_copy(step, g, lax.rem(row - step + n_row, n_row), g).wait_recv()
        wz_own(row, other).wait_recv()
        total = jnp.zeros((wr, half), f32)
        for r in range(n_row):
            for g in range(2):
                total = total + w_recv[r, g].astype(f32)
        w_all[w_rows(row, wr)] = total.astype(bf16)
        for step in range(1, n_row):
            wa_copy(step, row).start()

    def weight_cols():
        for step in range(1, n_row):
            wa_copy(step, lax.rem(row - step + n_row, n_row)).wait_recv()
        w_col[col] = w_all[w_rows(col, wc)]
        for k in range(1, n_col):
            wc_copy(k, col).start()

    def weight_final():
        for k in range(1, n_col):
            wc_copy(k, peer_from(k)).wait_recv()
        total = w_col[0].astype(f32)
        for c in range(1, n_col):
            total = total + w_col[c].astype(f32)
        w_fin[w_rows(col, wc)] = total
        for k in range(1, n_col):
            wf_copy(k, col).start()

    last = n_row - 1
    lower = row < n_row // 2
    inward = jnp.where(lower, row + 1, row - 1)
    outward = jnp.where(lower, row - 1, row + 1)
    depth = jnp.where(lower, n_row // 2 - 1 - row, row - n_row // 2)
    is_mid = depth == 0
    has_outer = (row > 0) & (row < last)
    steps = CHUNKS * pieces

    def to_sum(q):
        return remote(z_send.at[q], z_out.at[q], z_ssem.at[q], zo_rsem.at[q], {"row": inward})

    def to_cross(q):
        return remote(z_send.at[q], z_in.at[q], z_ssem.at[q], zi_rsem.at[q], {"row": inward})

    def to_final(q):
        return remote(z_fin.at[q], z_in.at[q], z_fsem.at[q], zi_rsem.at[q], {"row": outward})

    def store(p):
        at = pl.ds(pl.multiple_of(p * PIECE, PIECE), PIECE)
        return pltpu.make_async_copy(grad_input.at[at], grad_input_hbm.at[at], gin_sem.at[p])

    def chunk_arrived(ch):
        for h in range(PARTS):
            for k in range(n_col - 1, 0, -1):
                for g in range(2):
                    ag_copy(ch, k, g, h, block_of(peer_from(k), g, h)).wait_recv()
            own_ag(ch, h, other, block_of(col, other, h)).wait_recv()

    def contribute(q):
        ch, p = lax.div(q, pieces), lax.rem(q, pieces)

        @pl.when(p == 0)
        def _():
            chunk_arrived(ch)

        left = jnp.concatenate([grads[ch, s] for s in range(2 * n_col * PARTS)], axis=1)
        at = pl.ds(pl.multiple_of(p * PIECE, PIECE), PIECE)
        if cached:
            right = dense[:, at]
        else:
            wide = PIECE // blk

            def gather(rb, carry):
                for i in range(wide):
                    tile = which(rb * col_blocks + p * wide + i)
                    strip[pl.ds(pl.multiple_of(rb * blk, blk), blk), i * blk:(i + 1) * blk] = tiles[tile]
                return carry

            lax.fori_loop(0, n_col * sub, gather, 0)
            right = strip[...]
        part = jnp.dot(left, right, preferred_element_type=f32)

        @pl.when(has_outer)
        def _():
            to_sum(q).wait_recv()
            z_send[q] = (part + z_out[q].astype(f32)).astype(bf16)

        @pl.when(jnp.logical_not(has_outer))
        def _():
            z_send[q] = part.astype(bf16)

        @pl.when(is_mid)
        def _():
            to_cross(q).start()

        @pl.when(jnp.logical_not(is_mid))
        def _():
            to_sum(q).start()

    def finish(q):
        ch, p = lax.div(q, pieces), lax.rem(q, pieces)
        to_cross(q).wait_recv()

        @pl.when(is_mid)
        def _():
            z_fin[q] = (z_send[q].astype(f32) + z_in[q].astype(f32)).astype(bf16)

        @pl.when(jnp.logical_not(is_mid))
        def _():
            z_fin[q] = z_in[q]

        @pl.when(has_outer)
        def _():
            to_final(q).start()

        @pl.when(ch == CHUNKS - 1)
        def _():
            whole = jnp.concatenate([z_fin[c * pieces + p] for c in range(CHUNKS)], axis=0)
            grad_input[pl.ds(pl.multiple_of(p * PIECE, PIECE), PIECE)] = jnp.transpose(whole)
            store(p).start()

    lag = LAG + depth * LAG_STEP
    longest = LAG + (n_row // 2 - 1) * LAG_STEP
    at_rows = jnp.where(has_outer, 0, 4)
    at_cols = jnp.where(has_outer, 7, steps)
    at_final = jnp.where(has_outer, 11, steps + 2)

    def z_step(j, carry):
        @pl.when(j == at_rows)
        def _():
            weight_rows()

        @pl.when(j < steps)
        def _():
            contribute(j)

        @pl.when((j >= lag) & (j < steps + lag))
        def _():
            finish(j - lag)

        @pl.when(j == at_cols)
        def _():
            weight_cols()

        @pl.when(j == at_final)
        def _():
            weight_final()

        return carry

    lax.fori_loop(0, steps + longest, z_step, 0)

    for k in range(1, n_col):
        wf_copy(k, peer_from(k)).wait_recv()
    grad_weight[...] = w_fin[...] * scale + noise[...]
    of_copy.wait()
    outs = [
        pltpu.make_async_copy(out_feat, out_feat_hbm, out_sem.at[0]),
        pltpu.make_async_copy(grad_weight, grad_weight_hbm, out_sem.at[1]),
    ]
    for copy in outs:
        copy.start()

    for h in range(PARTS):
        own_copy(h, feat).wait_send()
        for ch in range(CHUNKS):
            own_ag(ch, h, other, block_of(col, feat, h)).wait_send()
        for k in range(1, n_col):
            for g in range(2):
                rs_copy(k, h, g, feat).wait_send()
                for ch in range(CHUNKS):
                    ag_copy(ch, k, g, h, block_of(col, feat, h)).wait_send()
    for step in range(1, n_row):
        for g in range(2):
            wz_copy(step, g, row, feat).wait_send()
        wa_copy(step, row).wait_send()
    wz_own(row, feat).wait_send()
    for k in range(1, n_col):
        wc_copy(k, col).wait_send()
        wf_copy(k, col).wait_send()

    def drain(q, carry):
        to_sum(q).wait_send()

        @pl.when(has_outer)
        def _():
            to_final(q).wait_send()

        return carry

    lax.fori_loop(0, steps, drain, 0)
    for p in range(pieces):
        store(p).wait()
    for copy in outs:
        copy.wait()


def deliver(a_in, b_in, c_in, a_out, b_out, c_out, a_buf, b_buf, c_buf, sems):
    rows = ((a_in, a_buf, a_out), (b_in, b_buf, b_out), (c_in, c_buf, c_out))
    loads = [pltpu.make_async_copy(src, buf, sems.at[0, i]) for i, (src, buf, _) in enumerate(rows)]
    stores = [pltpu.make_async_copy(buf, dst, sems.at[1, i]) for i, (_, buf, dst) in enumerate(rows)]
    for copy in loads:
        copy.start()
    for load, store in zip(loads, stores):
        load.wait()
        store.start()
    for copy in stores:
        copy.wait()


def per_device(
    tile_values, tile_rows, tile_cols, tile_mask, degree_caps, clip_groups,
    clip_bounds, features, weight, out_grad, dp_noise,
):
    tile_vals = tile_values[0, 0]
    slots, blk = tile_vals.shape[0], tile_vals.shape[1]
    node, half = out_grad.shape
    n_col, n_row = lax.axis_size("col"), lax.axis_size("row")
    col_range = features.shape[0]
    row_range = node * n_col
    hid = weight.shape[0]
    cached = row_range * col_range * 2 <= (20 << 20)
    pieces = col_range // PIECE
    places = -(-(row_range // blk) * (col_range // blk) // (8 * LANES)) * 8
    mine, nb, fc = node // 2, node // 2 // PARTS, half // CHUNKS
    wr, wc = hid // n_row, hid // n_col
    steps = CHUNKS * pieces
    bf16, f32, i32 = jnp.bfloat16, jnp.float32, jnp.int32
    anywhere = pl.BlockSpec(memory_space=pl.ANY)
    sem, vmem, smem = pltpu.SemaphoreType.DMA, pltpu.VMEM, pltpu.SMEM
    shapes = (
        jax.ShapeDtypeStruct((node, half), bf16),
        jax.ShapeDtypeStruct((hid, half), f32),
        jax.ShapeDtypeStruct((col_range, half), bf16),
    )
    call = pl.pallas_call(
        functools.partial(layer, n_row, n_col, 1.0 / math.sqrt(node * n_col * n_row), cached),
        out_shape=shapes,
        in_specs=[anywhere] * 11,
        out_specs=[anywhere] * 3,
        scratch_shapes=[
            smem((slots,), i32), smem((slots,), i32), smem((slots,), i32), smem(clip_bounds.shape, f32),
            smem((places, LANES), i32), vmem((places, LANES), i32),
            vmem((1, node), i32), vmem((1, node), i32),
            vmem((col_range, half), bf16),
            vmem((hid, hid), bf16),
            vmem((node, half), bf16),
            vmem((hid, half), f32),
            vmem((node, half), bf16),
            vmem((hid, half), f32),
            vmem((col_range, half), bf16),
            vmem((slots + 1, blk, blk), bf16),
            vmem((row_range if cached else node, col_range), bf16),
            vmem((16, LANES) if cached else (row_range, PIECE), bf16),
            vmem((n_col - 1, 2, PARTS, nb, half), bf16),
            vmem((n_col - 1, 2, PARTS, nb, half), bf16),
            vmem((2, PARTS, nb, half), f32),
            vmem((2, PARTS, nb, half), f32),
            vmem((mine, half), bf16),
            vmem((mine, LANES), f32),
            vmem((mine, LANES), f32),
            vmem((2, mine, half), bf16),
            vmem((2, CHUNKS, PARTS, fc, nb), bf16),
            vmem((CHUNKS, 2 * n_col * PARTS, fc, nb), bf16),
            vmem((2, n_row, wr, half), bf16),
            vmem((n_row, 2, wr, half), bf16),
            vmem((hid, half), bf16),
            vmem((n_col, wc, half), bf16),
            vmem((hid, half), f32),
            vmem((steps, fc, PIECE), bf16),
            vmem((steps, fc, PIECE), bf16),
            vmem((steps, fc, PIECE), bf16),
            vmem((steps, fc, PIECE), bf16),
            sem((6,)), sem((1,)), sem((LOADS,)), sem((4,)), sem((2,)), sem((pieces,)), sem((2,)),
            sem((2, PARTS)), sem((2,)),
            sem((n_col - 1, 2, PARTS)), sem((n_col - 1, 2, PARTS)),
            sem((CHUNKS, n_col - 1, 2, PARTS)), sem((CHUNKS, 2 * n_col * PARTS)), sem((CHUNKS, PARTS)),
            sem((n_row, 2)), sem((n_row, 2)), sem((n_row - 1,)), sem((n_row,)),
            sem((n_col - 1,)), sem((n_col,)), sem((n_col - 1,)), sem((n_col,)),
            sem((steps,)), sem((steps,)), sem((steps,)), sem((steps,)),
        ],
        compiler_params=pltpu.CompilerParams(
            collective_id=0, has_side_effects=True, vmem_limit_bytes=56 << 20
        ),
        name="layer",
    )
    results = call(
        tile_vals, tile_rows[0, 0], tile_cols[0, 0], tile_mask[0, 0],
        degree_caps[None, :], clip_groups[None, :], clip_bounds,
        features, weight, out_grad, dp_noise,
    )
    return pl.pallas_call(
        deliver,
        out_shape=shapes,
        in_specs=[anywhere] * 3,
        out_specs=[anywhere] * 3,
        scratch_shapes=[pltpu.VMEM(x.shape, x.dtype) for x in shapes] + [sem((2, 3))],
        name="deliver",
    )(*results)


def solution(mesh):
    placed = (
        P("row", "col", None, None, None),
        P("row", "col", None),
        P("row", "col", None),
        P("row", "col", None),
        P(("row", "col")),
        P(("row", "col")),
        P(),
        P("col", "feat"),
        P(),
        P(("row", "col"), "feat"),
        P(None, "feat"),
    )
    return jax.shard_map(
        per_device,
        mesh=mesh,
        in_specs=placed,
        out_specs=(P(("row", "col"), "feat"), P(None, "feat"), P("col", "feat")),
        check_vma=False,
    )
```

```python
import functools
import math

import jax
import jax.numpy as jnp
from jax import lax
from jax.experimental import pallas as pl
from jax.experimental.pallas import tpu as pltpu
from jax.sharding import PartitionSpec as P

MESH = pl.DeviceIdType.MESH
LANES = 128
PIECE = 256
CHUNKS = 2
PARTS = 2
LOADS = 4
LAG = 4
LAG_STEP = 12


def layer(
    n_row, n_col, scale, cached,
    tiles_hbm, rows_hbm, cols_hbm, mask_hbm, caps_hbm, groups_hbm, bounds_hbm,
    feats_hbm, weight_hbm, og_hbm, noise_hbm,
    out_feat, grad_weight, grad_input,
    rows_s, cols_s, mask_s, bounds_s, map_s, map_v, caps, groups,
    feats, weight, out_grad, noise, feat_peer,
    tiles, dense, strip, rs_send, rs_recv, own_send, chip_part, og_peer,
    scale_col, bound_col, feat_halves, back_t, grads,
    w_send, w_recv, w_part, w_col, w_row, w_fin,
    z_send, z_out, z_in, z_fin,
    small_sem, map_sem, tile_sem, in_sem, og_sem, own_sem, of_sem,
    rs_ssem, rs_rsem, ag_ssem, ag_rsem, own_ag_sem,
    wz_ssem, wz_rsem, wc_ssem, wc_rsem, wr_ssem, wr_rsem, wf_ssem, wf_rsem,
    z_ssem, z_fsem, zo_rsem, zi_rsem,
):
    row, col, feat = lax.axis_index("row"), lax.axis_index("col"), lax.axis_index("feat")
    other = 1 - feat
    f32, bf16 = jnp.float32, jnp.bfloat16
    slots, blk = tiles_hbm.shape[0], tiles_hbm.shape[1]
    node, half = og_hbm.shape
    col_range = feats.shape[0]
    col_blocks = col_range // blk
    sub = node // blk
    mine = node // 2
    nb = mine // PARTS
    hid = weight.shape[0]
    fc = half // CHUNKS
    pieces = col_range // PIECE
    side = math.isqrt(n_col)
    side = side if side * side == n_col else n_col
    col_x, col_y = lax.rem(col, side), lax.div(col, side)
    wr = hid // n_row
    wrc = wr // n_col

    def remote(src, dst, ssem, rsem, where):
        return pltpu.make_async_remote_copy(
            src_ref=src, dst_ref=dst, send_sem=ssem, recv_sem=rsem,
            device_id=where, device_id_type=MESH,
        )

    def peer_to(k):
        x, y = k % side, k // side
        return lax.rem(col_y + y, n_col // side) * side + lax.rem(col_x + x, side)

    def peer_from(k):
        x, y = k % side, k // side
        up = n_col // side
        return lax.rem(col_y - y + up, up) * side + lax.rem(col_x - x + side, side)

    small = [
        pltpu.make_async_copy(src, dst, small_sem.at[i])
        for i, (src, dst) in enumerate((
            (rows_hbm, rows_s), (cols_hbm, cols_s), (mask_hbm, mask_s), (bounds_hbm, bounds_s),
            (caps_hbm, caps), (groups_hbm, groups),
        ))
    ]
    count = slots // LOADS
    loads = [
        pltpu.make_async_copy(
            tiles_hbm.at[pl.ds(i * count, count)], tiles.at[pl.ds(i * count, count)], tile_sem.at[i]
        )
        for i in range(LOADS)
    ]
    inputs = [
        pltpu.make_async_copy(src, dst, in_sem.at[i])
        for i, (src, dst) in enumerate(
            ((feats_hbm, feats), (og_hbm, out_grad), (weight_hbm, weight), (noise_hbm, noise))
        )
    ]
    for copy in small + inputs[:1] + loads + inputs[1:]:
        copy.start()

    barrier = pltpu.get_barrier_semaphore()

    def greet(where):
        pl.semaphore_signal(barrier, inc=1, device_id=where, device_id_type=MESH)

    greet({"feat": other})
    for g in range(2):
        for k in range(1, n_col):
            greet({"col": peer_to(k), "feat": g})
        for step in range(1, n_row):
            greet({"row": lax.rem(row + step, n_row), "feat": g})

    tiles[slots] = jnp.zeros((blk, blk), bf16)
    for copy in small[:3]:
        copy.wait()
    spot = lax.broadcasted_iota(jnp.int32, map_v.shape, 0) * LANES + lax.broadcasted_iota(jnp.int32, map_v.shape, 1)

    def place(k, found):
        at = jnp.where(mask_s[k] == 1, rows_s[k] * col_blocks + cols_s[k], -1)
        return jnp.where(spot == at, k, found)

    map_v[...] = lax.fori_loop(0, slots, place, jnp.full(map_v.shape, slots, jnp.int32), unroll=8)
    map_copy = pltpu.make_async_copy(map_v, map_s, map_sem.at[0])
    map_copy.start()
    for copy in small[3:]:
        copy.wait()

    def column(values):
        return jnp.transpose(jnp.broadcast_to(values, (LANES, mine)))

    my_nodes = pl.ds(pl.multiple_of(feat * mine, mine), mine)
    scale_row = lax.rsqrt(caps[:, my_nodes].astype(f32))
    scale_col[...] = column(scale_row)
    bound = jnp.zeros((1, mine), f32)
    for g in range(bounds_s.shape[0]):
        bound = bound + jnp.where(groups[:, my_nodes] == g, bounds_s[g], 0.0)
    bound_col[...] = column(bound)
    map_copy.wait()
    inputs[0].wait()
    for copy in loads:
        copy.wait()

    def which(index):
        return map_s[index // LANES, index % LANES] if isinstance(index, int) else map_s[lax.div(index, LANES), lax.rem(index, LANES)]

    def assemble(chunk, h):
        base = chunk * node if cached else 0
        for g in range(2):
            for b in range(nb // blk):
                rb = (g * mine + h * nb) // blk + b
                at = pl.ds(pl.multiple_of(base + rb * blk, blk), blk)
                for cb in range(col_blocks):
                    tile = which((chunk * sub + rb) * col_blocks + cb)
                    dense[at, cb * blk:(cb + 1) * blk] = tiles[tile]

    def partial_sum(chunk, h):
        assemble(chunk, h)
        base = chunk * node if cached else 0
        left = jnp.concatenate(
            [dense[pl.ds(pl.multiple_of(base + g * mine + h * nb, blk), nb), :] for g in range(2)], axis=0
        )
        return jnp.dot(left, feats[...], preferred_element_type=f32)

    def rs_copy(k, h, g, sender):
        return remote(
            rs_send.at[k - 1, g, h], rs_recv.at[k - 1, sender, h],
            rs_ssem.at[k - 1, g, h], rs_rsem.at[k - 1, sender, h],
            {"col": peer_to(k), "feat": g},
        )

    def make(k, h):
        part = partial_sum(peer_to(k), h).astype(bf16)
        for g in range(2):
            rs_send[k - 1, g, h] = part[g * nb:(g + 1) * nb]

    def push(k, h):
        for g in range(2):
            rs_copy(k, h, g, feat).start()

    def own_copy(h, sender):
        return remote(
            own_send.at[1 - sender, h], chip_part.at[sender, h],
            own_sem.at[0, h], own_sem.at[1, h], {"feat": other},
        )

    def make_own(h):
        part = partial_sum(col, h)
        for g in range(2):
            own_send[g, h] = part[g * nb:(g + 1) * nb]
        own_copy(h, feat).start()
        chip_part[feat, h] = own_send[feat, h]

    make(n_col - 1, 0)
    pl.semaphore_wait(barrier, 2 * (n_col + n_row) - 3)
    push(n_col - 1, 0)
    for copy in inputs[1:]:
        copy.wait()
    theirs = pl.ds(pl.multiple_of(other * mine, mine), mine)
    og_copy = remote(out_grad.at[theirs], og_peer, og_sem.at[0], og_sem.at[1], {"feat": other})
    og_copy.start()

    for h in range(PARTS):
        def forward(i, carry):
            k = n_col - 1 - i
            make(k, h)
            push(k, h)
            return carry

        lax.fori_loop(1 if h == 0 else 0, n_col - 1, forward, 0)
        make_own(h)

    def block_of(c, g, h):
        return (c * 2 + g) * PARTS + h

    def ag_copy(ch, k, g, h, sender):
        return remote(
            back_t.at[g, ch, h], grads.at[ch, sender],
            ag_ssem.at[ch, k - 1, g, h], ag_rsem.at[ch, sender], {"col": peer_to(k), "feat": g},
        )

    def own_ag(ch, h, g, sender):
        return remote(
            back_t.at[g, ch, h], grads.at[ch, sender],
            own_ag_sem.at[ch, h], ag_rsem.at[ch, sender], {"feat": other},
        )

    w_total = jnp.zeros((hid, hid), f32)
    og_copy.wait_recv()
    for h in range(PARTS):
        spot_h = slice(h * nb, (h + 1) * nb)
        own_copy(h, other).wait_recv()
        sums = [chip_part[0, h], chip_part[1, h]]
        for k in range(n_col - 1, 0, -1):
            for g in range(2):
                rs_copy(k, h, g, g).wait_recv()
                sums[g] = sums[g] + rs_recv[k - 1, g, h].astype(f32)
        node_scale = scale_col[spot_h]
        agg = jnp.concatenate([(s * node_scale).astype(bf16) for s in sums], axis=1)
        here = pl.ds(pl.multiple_of(feat * mine + h * nb, nb), nb)
        mine_og = out_grad[here]
        peer_og = og_peer[spot_h]
        cotangent = jnp.concatenate(
            [jnp.where(feat == 0, mine_og, peer_og), jnp.where(feat == 0, peer_og, mine_og)], axis=1
        )
        pre = jnp.dot(agg, weight[...], preferred_element_type=f32)
        sig = 1.0 / (1.0 + jnp.exp(-pre))
        grad = (cotangent.astype(f32) * sig * (1.0 + pre * (1.0 - sig))).astype(bf16)
        back = lax.dot_general(grad, weight[...], (((1,), (1,)), ((), ())), preferred_element_type=f32)
        back = (jnp.transpose(back) * scale_row[:, spot_h]).astype(bf16)
        for g in range(2):
            for ch in range(CHUNKS):
                at = g * half + ch * fc
                back_t[g, ch, h] = back[at:at + fc]
        me = block_of(col, feat, h)
        for ch in range(CHUNKS):
            for k in range(n_col - 1, 0, -1):
                for g in range(2):
                    ag_copy(ch, k, g, h, me).start()
            own_ag(ch, h, other, me).start()
            grads[ch, me] = back_t[feat, ch, h]
        activated = (pre * sig).astype(bf16)
        for g in range(2):
            feat_halves[g, h * nb:(h + 1) * nb] = activated[:, g * half:(g + 1) * half]

        def norm(value):
            value = value.astype(f32)
            return jnp.sqrt(jnp.sum(value * value, axis=1, keepdims=True) + 1e-06)

        factor = jnp.minimum(1.0, bound_col[spot_h] / (norm(agg) * norm(grad)))
        wide = grad.astype(f32)
        clipped = jnp.concatenate(
            [(factor * wide[:, g * half:(g + 1) * half]).astype(bf16) for g in range(2)], axis=1
        )
        w_total = w_total + lax.dot_general(agg, clipped, (((0,), (0,)), ((), ())), preferred_element_type=f32)

    def wz_copy(step, g, r, s):
        return remote(
            w_send.at[g, lax.rem(row + step, n_row)], w_recv.at[r, s],
            wz_ssem.at[step, g], wz_rsem.at[r, s], {"row": lax.rem(row + step, n_row), "feat": g},
        )

    def wz_own(r, s):
        return remote(
            w_send.at[other, row], w_recv.at[r, s], wz_ssem.at[0, 0], wz_rsem.at[r, s], {"feat": other}
        )

    for g in range(2):
        for r in range(n_row):
            w_send[g, r] = w_total[r * wr:(r + 1) * wr, g * half:(g + 1) * half].astype(bf16)
    w_recv[row, feat] = w_send[feat, row]
    for step in range(1, n_row):
        for g in range(2):
            wz_copy(step, g, row, feat).start()
    wz_own(row, feat).start()

    of_copy = remote(feat_halves.at[other], feat_peer, of_sem.at[0], of_sem.at[1], {"feat": other})
    of_copy.start()
    kept = pl.ds(pl.multiple_of(feat * mine, mine), mine)
    out_feat[kept] = feat_halves[feat]

    def wc_copy(k, sender):
        return remote(
            w_part.at[peer_to(k)], w_col.at[sender], wc_ssem.at[k - 1], wc_rsem.at[sender], {"col": peer_to(k)}
        )

    def wr_copy(step, sender):
        spot = w_row.at[sender]
        return remote(spot, spot, wr_ssem.at[step - 1], wr_rsem.at[sender], {"row": lax.rem(row + step, n_row)})

    def wf_copy(k, sender):
        spot = w_fin.at[sender]
        return remote(spot, spot, wf_ssem.at[k - 1], wf_rsem.at[sender], {"col": peer_to(k)})

    def weight_rows():
        for step in range(1, n_row):
            for g in range(2):
                wz_copy(step, g, lax.rem(row - step + n_row, n_row), g).wait_recv()
        wz_own(row, other).wait_recv()
        total = jnp.zeros((wr, half), f32)
        for r in range(n_row):
            for g in range(2):
                total = total + w_recv[r, g].astype(f32)
        for c in range(n_col):
            w_part[c] = total[c * wrc:(c + 1) * wrc]
        for k in range(1, n_col):
            wc_copy(k, col).start()
        w_col[col] = w_part[col]

    def weight_cols():
        for k in range(1, n_col):
            wc_copy(k, peer_from(k)).wait_recv()
        total = w_col[0]
        for c in range(1, n_col):
            total = total + w_col[c]
        w_row[row] = total
        for step in range(1, n_row):
            wr_copy(step, row).start()

    def weight_spread():
        for step in range(1, n_row):
            wr_copy(step, lax.rem(row - step + n_row, n_row)).wait_recv()
        w_fin[col] = w_row[...]
        for k in range(1, n_col):
            wf_copy(k, col).start()

    def settle():
        of_copy.wait()
        out_feat[theirs] = feat_peer[...]
        og_copy.wait_send()
        for h in range(PARTS):
            own_copy(h, feat).wait_send()
            for ch in range(CHUNKS):
                own_ag(ch, h, other, block_of(col, feat, h)).wait_send()
            for k in range(1, n_col):
                for g in range(2):
                    rs_copy(k, h, g, feat).wait_send()
                    for ch in range(CHUNKS):
                        ag_copy(ch, k, g, h, block_of(col, feat, h)).wait_send()
        for step in range(1, n_row):
            for g in range(2):
                wz_copy(step, g, row, feat).wait_send()
        wz_own(row, feat).wait_send()

    last = n_row - 1
    lower = row < n_row // 2
    inward = jnp.where(lower, row + 1, row - 1)
    outward = jnp.where(lower, row - 1, row + 1)
    depth = jnp.where(lower, n_row // 2 - 1 - row, row - n_row // 2)
    is_mid = depth == 0
    has_outer = (row > 0) & (row < last)
    steps = CHUNKS * pieces

    def to_sum(q):
        return remote(z_send.at[q], z_out.at[q], z_ssem.at[0], zo_rsem.at[q], {"row": inward})

    def to_cross(q):
        return remote(z_send.at[q], z_in.at[q], z_ssem.at[0], zi_rsem.at[q], {"row": inward})

    def to_final(q):
        return remote(z_fin.at[q], z_in.at[q], z_fsem.at[0], zi_rsem.at[q], {"row": outward})

    def chunk_arrived(ch):
        for h in range(PARTS):
            for k in range(n_col - 1, 0, -1):
                for g in range(2):
                    ag_copy(ch, k, g, h, block_of(peer_from(k), g, h)).wait_recv()
            own_ag(ch, h, other, block_of(col, other, h)).wait_recv()

    def contribute(q):
        ch, p = lax.div(q, pieces), lax.rem(q, pieces)

        @pl.when(p == 0)
        def _():
            chunk_arrived(ch)

        left = jnp.concatenate([grads[ch, s] for s in range(2 * n_col * PARTS)], axis=1)
        at = pl.ds(pl.multiple_of(p * PIECE, PIECE), PIECE)
        if cached:
            right = dense[:, at]
        else:
            wide = PIECE // blk

            def gather(rb, carry):
                for i in range(wide):
                    tile = which(rb * col_blocks + p * wide + i)
                    strip[pl.ds(pl.multiple_of(rb * blk, blk), blk), i * blk:(i + 1) * blk] = tiles[tile]
                return carry

            lax.fori_loop(0, n_col * sub, gather, 0)
            right = strip[...]
        part = jnp.dot(left, right, preferred_element_type=f32)

        @pl.when(has_outer)
        def _():
            to_sum(q).wait_recv()
            z_send[q] = (part + z_out[q].astype(f32)).astype(bf16)

        @pl.when(jnp.logical_not(has_outer))
        def _():
            z_send[q] = part.astype(bf16)

        @pl.when(is_mid)
        def _():
            to_cross(q).start()

        @pl.when(jnp.logical_not(is_mid))
        def _():
            to_sum(q).start()

    def finish(q):
        ch, p = lax.div(q, pieces), lax.rem(q, pieces)
        to_cross(q).wait_recv()

        @pl.when(is_mid)
        def _():
            z_fin[q] = (z_send[q].astype(f32) + z_in[q].astype(f32)).astype(bf16)

        @pl.when(jnp.logical_not(is_mid))
        def _():
            z_fin[q] = z_in[q]

        @pl.when(has_outer)
        def _():
            to_final(q).start()

        @pl.when(ch == CHUNKS - 1)
        def _():
            whole = jnp.concatenate([z_fin[c * pieces + p] for c in range(CHUNKS)], axis=0)
            grad_input[pl.ds(pl.multiple_of(p * PIECE, PIECE), PIECE)] = jnp.transpose(whole)

    lag = LAG + depth * LAG_STEP
    longest = LAG + (n_row // 2 - 1) * LAG_STEP
    stages = (
        (weight_rows, 1, 3), (weight_cols, 5, 7), (weight_spread, 14, 18), (settle, 15, 19)
    )

    def z_step(j, carry):
        @pl.when(j < steps)
        def _():
            contribute(j)

        @pl.when((j >= lag) & (j < steps + lag))
        def _():
            finish(j - lag)

        for stage, inner, outer in stages:
            pl.when(j == jnp.where(has_outer, inner, outer))(stage)

        return carry

    lax.fori_loop(0, steps + longest, z_step, 0)

    for k in range(1, n_col):
        wf_copy(k, peer_from(k)).wait_recv()
    for c in range(n_col):
        for r in range(n_row):
            at = r * wr + c * wrc
            grad_weight[at:at + wrc] = w_fin[c, r] * scale + noise[at:at + wrc]

    for step in range(1, n_row):
        wr_copy(step, row).wait_send()
    for k in range(1, n_col):
        wc_copy(k, col).wait_send()
        wf_copy(k, col).wait_send()
    remote(z_send, z_out, z_ssem.at[0], zo_rsem.at[0], {"row": inward}).wait_send()

    @pl.when(has_outer)
    def _():
        remote(z_fin, z_in, z_fsem.at[0], zi_rsem.at[0], {"row": outward}).wait_send()


def deliver(a_in, b_in, c_in, a_out, b_out, c_out, sems):
    pairs = ((a_in, a_out), (b_in, b_out), (c_in, c_out))
    stores = [pltpu.make_async_copy(src, dst, sems.at[i]) for i, (src, dst) in enumerate(pairs)]
    for copy in stores:
        copy.start()
    for copy in stores:
        copy.wait()


def per_device(
    tile_values, tile_rows, tile_cols, tile_mask, degree_caps, clip_groups,
    clip_bounds, features, weight, out_grad, dp_noise,
):
    tile_vals = tile_values[0, 0]
    slots, blk = tile_vals.shape[0], tile_vals.shape[1]
    node, half = out_grad.shape
    n_col, n_row = lax.axis_size("col"), lax.axis_size("row")
    col_range = features.shape[0]
    row_range = node * n_col
    hid = weight.shape[0]
    cached = row_range * col_range * 2 <= (20 << 20)
    pieces = col_range // PIECE
    places = -(-(row_range // blk) * (col_range // blk) // (8 * LANES)) * 8
    mine, nb, fc = node // 2, node // 2 // PARTS, half // CHUNKS
    wr, wrc = hid // n_row, hid // n_row // n_col
    steps = CHUNKS * pieces
    bf16, f32, i32 = jnp.bfloat16, jnp.float32, jnp.int32
    anywhere = pl.BlockSpec(memory_space=pl.ANY)
    sem, vmem, smem = pltpu.SemaphoreType.DMA, pltpu.VMEM, pltpu.SMEM
    shapes = (
        jax.ShapeDtypeStruct((node, half), bf16),
        jax.ShapeDtypeStruct((hid, half), f32),
        jax.ShapeDtypeStruct((col_range, half), bf16),
    )
    call = pl.pallas_call(
        functools.partial(layer, n_row, n_col, 1.0 / math.sqrt(node * n_col * n_row), cached),
        out_shape=tuple(pltpu.VMEM(x.shape, x.dtype) for x in shapes),
        in_specs=[anywhere] * 11,
        out_specs=[pl.BlockSpec(memory_space=pltpu.VMEM)] * 3,
        scratch_shapes=[
            smem((slots,), i32), smem((slots,), i32), smem((slots,), i32), smem(clip_bounds.shape, f32),
            smem((places, LANES), i32), vmem((places, LANES), i32),
            vmem((1, node), i32), vmem((1, node), i32),
            vmem((col_range, half), bf16),
            vmem((hid, hid), bf16),
            vmem((node, half), bf16),
            vmem((hid, half), f32),
            vmem((mine, half), bf16),
            vmem((slots + 1, blk, blk), bf16),
            vmem((row_range if cached else node, col_range), bf16),
            vmem((16, LANES) if cached else (row_range, PIECE), bf16),
            vmem((n_col - 1, 2, PARTS, nb, half), bf16),
            vmem((n_col - 1, 2, PARTS, nb, half), bf16),
            vmem((2, PARTS, nb, half), f32),
            vmem((2, PARTS, nb, half), f32),
            vmem((mine, half), bf16),
            vmem((mine, LANES), f32),
            vmem((mine, LANES), f32),
            vmem((2, mine, half), bf16),
            vmem((2, CHUNKS, PARTS, fc, nb), bf16),
            vmem((CHUNKS, 2 * n_col * PARTS, fc, nb), bf16),
            vmem((2, n_row, wr, half), bf16),
            vmem((n_row, 2, wr, half), bf16),
            vmem((n_col, wrc, half), f32),
            vmem((n_col, wrc, half), f32),
            vmem((n_row, wrc, half), f32),
            vmem((n_col, n_row, wrc, half), f32),
            vmem((steps, fc, PIECE), bf16),
            vmem((steps, fc, PIECE), bf16),
            vmem((steps, fc, PIECE), bf16),
            vmem((steps, fc, PIECE), bf16),
            sem((6,)), sem((1,)), sem((LOADS,)), sem((4,)), sem((2,)),
            sem((2, PARTS)), sem((2,)),
            sem((n_col - 1, 2, PARTS)), sem((n_col - 1, 2, PARTS)),
            sem((CHUNKS, n_col - 1, 2, PARTS)), sem((CHUNKS, 2 * n_col * PARTS)), sem((CHUNKS, PARTS)),
            sem((n_row, 2)), sem((n_row, 2)), sem((n_col - 1,)), sem((n_col,)),
            sem((n_row - 1,)), sem((n_row,)), sem((n_col - 1,)), sem((n_col,)),
            sem((1,)), sem((1,)), sem((steps,)), sem((steps,)),
        ],
        compiler_params=pltpu.CompilerParams(
            collective_id=0, has_side_effects=True, vmem_limit_bytes=56 << 20
        ),
        name="layer",
    )
    results = call(
        tile_vals, tile_rows[0, 0], tile_cols[0, 0], tile_mask[0, 0],
        degree_caps[None, :], clip_groups[None, :], clip_bounds,
        features, weight, out_grad, dp_noise,
    )
    return pl.pallas_call(
        deliver,
        out_shape=shapes,
        in_specs=[pl.BlockSpec(memory_space=pltpu.VMEM)] * 3,
        out_specs=[anywhere] * 3,
        scratch_shapes=[sem((3,))],
        compiler_params=pltpu.CompilerParams(vmem_limit_bytes=4 << 20),
        name="deliver",
    )(*results)


def solution(mesh):
    placed = (
        P("row", "col", None, None, None),
        P("row", "col", None),
        P("row", "col", None),
        P("row", "col", None),
        P(("row", "col")),
        P(("row", "col")),
        P(),
        P("col", "feat"),
        P(),
        P(("row", "col"), "feat"),
        P(None, "feat"),
    )
    return jax.shard_map(
        per_device,
        mesh=mesh,
        in_specs=placed,
        out_specs=(P(("row", "col"), "feat"), P(None, "feat"), P("col", "feat")),
        check_vma=False,
    )
```

```python
import functools
import math

import jax
import jax.numpy as jnp
from jax import lax
from jax.experimental import pallas as pl
from jax.experimental.pallas import tpu as pltpu
from jax.sharding import PartitionSpec as P

MESH = pl.DeviceIdType.MESH
LANES = 128
PIECE = 256
CHUNKS = 2
PARTS = 2
LOADS = 2
LAG = 4
LAG_STEP = 12
MOVED = 2
GUEST_AT = 7
HOSTS = 3


def layer(
    n_row, n_col, scale, cached,
    tiles_hbm, rows_hbm, cols_hbm, mask_hbm, caps_hbm, groups_hbm, bounds_hbm,
    feats_hbm, weight_hbm, og_hbm, noise_hbm,
    out_feat, grad_weight, grad_input,
    rows_s, cols_s, mask_s, bounds_s, map_s, map_v, caps, groups,
    feats, weight, out_grad, noise, feat_peer,
    tiles, dense, strip, rs_send, rs_recv, own_send, chip_part, cotangents,
    scale_col, bound_col, feat_halves, back_t, grads,
    w_send, w_recv, w_part, w_col, w_row, w_fin,
    own_part, guest_send, guest_in, z_send, z_out, z_in, z_fin,
    small_sem, map_sem, tile_sem, in_sem, og_sem, own_sem, of_sem,
    rs_ssem, rs_rsem, ag_ssem, ag_rsem, own_ag_sem,
    wz_ssem, wz_rsem, wc_ssem, wc_rsem, wr_ssem, wr_rsem, wf_ssem, wf_rsem,
    z_ssem, z_fsem, zo_rsem, zi_rsem, guest_ssem, guest_rsem, back_ssem, back_rsem,
):
    row, col, feat = lax.axis_index("row"), lax.axis_index("col"), lax.axis_index("feat")
    other = 1 - feat
    f32, bf16 = jnp.float32, jnp.bfloat16
    slots, blk = tiles_hbm.shape[0], tiles_hbm.shape[1]
    node, half = og_hbm.shape
    col_range = feats.shape[0]
    col_blocks = col_range // blk
    sub = node // blk
    mine = node // 2
    nb = mine // PARTS
    hid = weight.shape[0]
    fc = half // CHUNKS
    pieces = col_range // PIECE
    side = math.isqrt(n_col)
    side = side if side * side == n_col else n_col
    col_x, col_y = lax.rem(col, side), lax.div(col, side)
    wr = hid // n_row
    wrc = wr // n_col

    def remote(src, dst, ssem, rsem, where):
        return pltpu.make_async_remote_copy(
            src_ref=src, dst_ref=dst, send_sem=ssem, recv_sem=rsem,
            device_id=where, device_id_type=MESH,
        )

    def peer_to(k):
        x, y = k % side, k // side
        return lax.rem(col_y + y, n_col // side) * side + lax.rem(col_x + x, side)

    def peer_from(k):
        x, y = k % side, k // side
        up = n_col // side
        return lax.rem(col_y - y + up, up) * side + lax.rem(col_x - x + side, side)

    small = [
        pltpu.make_async_copy(src, dst, small_sem.at[i])
        for i, (src, dst) in enumerate((
            (rows_hbm, rows_s), (cols_hbm, cols_s), (mask_hbm, mask_s), (bounds_hbm, bounds_s),
            (caps_hbm, caps), (groups_hbm, groups),
        ))
    ]
    count = slots // LOADS
    loads = [
        pltpu.make_async_copy(
            tiles_hbm.at[pl.ds(i * count, count)], tiles.at[pl.ds(i * count, count)], tile_sem.at[i]
        )
        for i in range(LOADS)
    ]
    inputs = [
        pltpu.make_async_copy(src, dst, in_sem.at[i])
        for i, (src, dst) in enumerate(
            ((feats_hbm, feats), (og_hbm, out_grad), (weight_hbm, weight), (noise_hbm, noise))
        )
    ]
    for copy in loads + inputs[:1] + small:
        copy.start()

    barrier = pltpu.get_barrier_semaphore()

    def greet(where):
        pl.semaphore_signal(barrier, inc=1, device_id=where, device_id_type=MESH)

    greet({"feat": other})
    for g in range(2):
        for k in range(1, n_col):
            greet({"col": peer_to(k), "feat": g})
        for step in range(1, n_row):
            greet({"row": lax.rem(row + step, n_row), "feat": g})

    for copy in inputs[1:]:
        copy.start()
    tiles[slots] = jnp.zeros((blk, blk), bf16)
    for copy in small[:3]:
        copy.wait()
    spot = lax.broadcasted_iota(jnp.int32, map_v.shape, 0) * LANES + lax.broadcasted_iota(jnp.int32, map_v.shape, 1)

    def place(k, found):
        at = jnp.where(mask_s[k] == 1, rows_s[k] * col_blocks + cols_s[k], -1)
        return jnp.where(spot == at, k, found)

    map_v[...] = lax.fori_loop(0, slots, place, jnp.full(map_v.shape, slots, jnp.int32), unroll=8)
    map_copy = pltpu.make_async_copy(map_v, map_s, map_sem.at[0])
    map_copy.start()
    for copy in small[3:]:
        copy.wait()

    def column(values):
        return jnp.transpose(jnp.broadcast_to(values, (LANES, mine)))

    my_nodes = pl.ds(pl.multiple_of(feat * mine, mine), mine)
    scale_row = lax.rsqrt(caps[:, my_nodes].astype(f32))
    scale_col[...] = column(scale_row)
    bound = jnp.zeros((1, mine), f32)
    for g in range(bounds_s.shape[0]):
        bound = bound + jnp.where(groups[:, my_nodes] == g, bounds_s[g], 0.0)
    bound_col[...] = column(bound)
    map_copy.wait()
    inputs[0].wait()
    for copy in loads:
        copy.wait()

    def which(index):
        return map_s[index // LANES, index % LANES] if isinstance(index, int) else map_s[lax.div(index, LANES), lax.rem(index, LANES)]

    def assemble(chunk, h, groups_of):
        base = chunk * node if cached else 0
        for g in groups_of:
            for b in range(nb // blk):
                rb = (g * mine + h * nb) // blk + b
                at = pl.ds(pl.multiple_of(base + rb * blk, blk), blk)
                for cb in range(col_blocks):
                    tile = which((chunk * sub + rb) * col_blocks + cb)
                    dense[at, cb * blk:(cb + 1) * blk] = tiles[tile]

    def partial_sum(chunk, h, groups_of=(0, 1)):
        assemble(chunk, h, groups_of)
        base = chunk * node if cached else 0
        left = jnp.concatenate(
            [dense[pl.ds(pl.multiple_of(base + g * mine + h * nb, blk), nb), :] for g in groups_of], axis=0
        )
        return jnp.dot(left, feats[...], preferred_element_type=f32)

    def rs_copy(k, h, g, sender):
        return remote(
            rs_send.at[k - 1, g, h], rs_recv.at[k - 1, sender, h],
            rs_ssem.at[k - 1, g, h], rs_rsem.at[k - 1, sender, h],
            {"col": peer_to(k), "feat": g},
        )

    def make(k, h):
        part = partial_sum(peer_to(k), h).astype(bf16)
        for g in range(2):
            rs_send[k - 1, g, h] = part[g * nb:(g + 1) * nb]

    def push(k, h):
        for g in range(2):
            rs_copy(k, h, g, feat).start()

    def own_copy(h, sender):
        return remote(
            own_send.at[1 - sender, h], chip_part.at[sender, h],
            own_sem.at[0, h], own_sem.at[1, h], {"feat": other},
        )

    def make_own(h):
        part = partial_sum(col, h)
        for g in range(2):
            own_send[g, h] = part[g * nb:(g + 1) * nb]
        own_copy(h, feat).start()
        chip_part[feat, h] = own_send[feat, h]

    for g in range(2):
        rs_send[n_col - 2, g, 0] = partial_sum(peer_to(n_col - 1), 0, (g,)).astype(bf16)
        if g == 0:
            pl.semaphore_wait(barrier, 2 * (n_col + n_row) - 3)
        rs_copy(n_col - 1, 0, g, feat).start()
    for copy in inputs[1:]:
        copy.wait()
    theirs = pl.ds(pl.multiple_of(other * mine, mine), mine)
    og_copy = remote(out_grad.at[theirs], cotangents.at[feat], og_sem.at[0], og_sem.at[1], {"feat": other})
    og_copy.start()

    for h in range(PARTS):
        def forward(i, carry):
            k = n_col - 1 - i
            make(k, h)
            push(k, h)
            return carry

        lax.fori_loop(1 if h == 0 else 0, n_col - 1, forward, 0)
        make_own(h)

    def block_of(c, g, h):
        return (c * 2 + g) * PARTS + h

    def ag_copy(ch, k, g, h, sender):
        return remote(
            back_t.at[g, ch, h], grads.at[ch, sender],
            ag_ssem.at[ch, k - 1, g, h], ag_rsem.at[ch, sender], {"col": peer_to(k), "feat": g},
        )

    def own_ag(ch, h, g, sender):
        return remote(
            back_t.at[g, ch, h], grads.at[ch, sender],
            own_ag_sem.at[ch, h], ag_rsem.at[ch, sender], {"feat": other},
        )

    w_total = jnp.zeros((hid, hid), f32)
    remote(out_grad.at[theirs], cotangents.at[other], og_sem.at[0], og_sem.at[1], {"feat": other}).wait_recv()
    cotangents[feat] = out_grad[pl.ds(pl.multiple_of(feat * mine, mine), mine)]
    for h in range(PARTS):
        spot_h = slice(h * nb, (h + 1) * nb)
        own_copy(h, other).wait_recv()
        sums = [chip_part[0, h], chip_part[1, h]]
        for k in range(n_col - 1, 0, -1):
            for g in range(2):
                rs_copy(k, h, g, g).wait_recv()
                sums[g] = sums[g] + rs_recv[k - 1, g, h].astype(f32)
        node_scale = scale_col[spot_h]
        agg = jnp.concatenate([(s * node_scale).astype(bf16) for s in sums], axis=1)
        cotangent = jnp.concatenate([cotangents[0, spot_h], cotangents[1, spot_h]], axis=1)
        pre = jnp.dot(agg, weight[...], preferred_element_type=f32)
        sig = 1.0 / (1.0 + jnp.exp(-pre))
        grad = (cotangent.astype(f32) * sig * (1.0 + pre * (1.0 - sig))).astype(bf16)
        me = block_of(col, feat, h)
        for ch in range(CHUNKS):
            rows = jnp.concatenate([weight[g * half + ch * fc:g * half + (ch + 1) * fc] for g in range(2)], axis=0)
            back = lax.dot_general(rows, grad, (((1,), (1,)), ((), ())), preferred_element_type=f32)
            back = (back * scale_row[:, spot_h]).astype(bf16)
            for g in range(2):
                back_t[g, ch, h] = back[g * fc:(g + 1) * fc]
            for k in range(n_col - 1, 0, -1):
                for g in range(2):
                    ag_copy(ch, k, g, h, me).start()
            own_ag(ch, h, other, me).start()
            grads[ch, me] = back_t[feat, ch, h]
        activated = (pre * sig).astype(bf16)
        for g in range(2):
            feat_halves[g, h * nb:(h + 1) * nb] = activated[:, g * half:(g + 1) * half]

        def norm(value):
            value = value.astype(f32)
            return jnp.sqrt(jnp.sum(value * value, axis=1, keepdims=True) + 1e-06)

        factor = jnp.minimum(1.0, bound_col[spot_h] / (norm(agg) * norm(grad)))
        wide = grad.astype(f32)
        clipped = jnp.concatenate(
            [(factor * wide[:, g * half:(g + 1) * half]).astype(bf16) for g in range(2)], axis=1
        )
        w_total = w_total + lax.dot_general(agg, clipped, (((0,), (0,)), ((), ())), preferred_element_type=f32)

    def wz_copy(step, g, r, s):
        return remote(
            w_send.at[g, lax.rem(row + step, n_row)], w_recv.at[r, s],
            wz_ssem.at[step, g], wz_rsem.at[r, s], {"row": lax.rem(row + step, n_row), "feat": g},
        )

    def wz_own(r, s):
        return remote(
            w_send.at[other, row], w_recv.at[r, s], wz_ssem.at[0, 0], wz_rsem.at[r, s], {"feat": other}
        )

    for g in range(2):
        for r in range(n_row):
            w_send[g, r] = w_total[r * wr:(r + 1) * wr, g * half:(g + 1) * half].astype(bf16)
    w_recv[row, feat] = w_send[feat, row]
    for step in range(1, n_row):
        for g in range(2):
            wz_copy(step, g, row, feat).start()
    wz_own(row, feat).start()

    of_copy = remote(feat_halves.at[other], feat_peer, of_sem.at[0], of_sem.at[1], {"feat": other})
    of_copy.start()
    kept = pl.ds(pl.multiple_of(feat * mine, mine), mine)
    out_feat[kept] = feat_halves[feat]

    def wc_copy(k, sender):
        return remote(
            w_part.at[peer_to(k)], w_col.at[sender], wc_ssem.at[k - 1], wc_rsem.at[sender], {"col": peer_to(k)}
        )

    def wr_copy(step, sender):
        spot = w_row.at[sender]
        return remote(spot, spot, wr_ssem.at[step - 1], wr_rsem.at[sender], {"row": lax.rem(row + step, n_row)})

    def wf_copy(k, sender):
        spot = w_fin.at[sender]
        return remote(spot, spot, wf_ssem.at[k - 1], wf_rsem.at[sender], {"col": peer_to(k)})

    def weight_rows():
        for step in range(1, n_row):
            for g in range(2):
                wz_copy(step, g, lax.rem(row - step + n_row, n_row), g).wait_recv()
        wz_own(row, other).wait_recv()
        total = jnp.zeros((wr, half), f32)
        for r in range(n_row):
            for g in range(2):
                total = total + w_recv[r, g].astype(f32)
        for c in range(n_col):
            w_part[c] = total[c * wrc:(c + 1) * wrc]
        for k in range(1, n_col):
            wc_copy(k, col).start()
        w_col[col] = w_part[col]

    def weight_cols():
        for k in range(1, n_col):
            wc_copy(k, peer_from(k)).wait_recv()
        total = w_col[0]
        for c in range(1, n_col):
            total = total + w_col[c]
        w_row[row] = total
        for step in range(1, n_row):
            wr_copy(step, row).start()

    def weight_spread():
        for step in range(1, n_row):
            wr_copy(step, lax.rem(row - step + n_row, n_row)).wait_recv()
        w_fin[col] = w_row[...]
        for k in range(1, n_col):
            wf_copy(k, col).start()

    def settle():
        of_copy.wait()
        out_feat[theirs] = feat_peer[...]
        og_copy.wait_send()
        for h in range(PARTS):
            own_copy(h, feat).wait_send()
            for ch in range(CHUNKS):
                own_ag(ch, h, other, block_of(col, feat, h)).wait_send()
            for k in range(1, n_col):
                for g in range(2):
                    rs_copy(k, h, g, feat).wait_send()
                    for ch in range(CHUNKS):
                        ag_copy(ch, k, g, h, block_of(col, feat, h)).wait_send()
        for step in range(1, n_row):
            for g in range(2):
                wz_copy(step, g, row, feat).wait_send()
        wz_own(row, feat).wait_send()

    def weight_done():
        for k in range(1, n_col):
            wf_copy(k, peer_from(k)).wait_recv()
        for c in range(n_col):
            for r in range(n_row):
                at = r * wr + c * wrc
                grad_weight[at:at + wrc] = w_fin[c, r] * scale + noise[at:at + wrc]
        for step in range(1, n_row):
            wr_copy(step, row).wait_send()
        for k in range(1, n_col):
            wc_copy(k, col).wait_send()
            wf_copy(k, col).wait_send()

    last = n_row - 1
    lower = row < n_row // 2
    inward = jnp.where(lower, row + 1, row - 1)
    outward = jnp.where(lower, row - 1, row + 1)
    depth = jnp.where(lower, n_row // 2 - 1 - row, row - n_row // 2)
    is_mid = depth == 0
    has_outer = (row > 0) & (row < last)
    steps = CHUNKS * pieces
    moved = MOVED if n_col > HOSTS else 0
    kept_here = pieces - moved
    home = col == 0 if moved else col < 0
    guest = (col > HOSTS - moved) & (col <= HOSTS)
    total = jnp.where(home, steps - moved, jnp.where(guest, steps + 1, steps))

    def piece_at(j):
        late = jnp.where(j == GUEST_AT, steps, j - 1)
        own = jnp.where(j < kept_here, j, j + moved)
        return jnp.where(home, own, jnp.where(guest & (j >= GUEST_AT), late, j))

    def lend(m):
        return remote(
            guest_send.at[m], guest_in.at[0], guest_ssem.at[m], guest_rsem.at[0], {"col": HOSTS - m}
        )

    def give_back(m):
        return remote(z_fin.at[steps], z_fin.at[kept_here + m], back_ssem.at[0], back_rsem.at[m], {"col": 0})

    def to_sum(q):
        return remote(z_send.at[q], z_out.at[q], z_ssem.at[0], zo_rsem.at[q], {"row": inward})

    def to_cross(q):
        return remote(z_send.at[q], z_in.at[q], z_ssem.at[0], zi_rsem.at[q], {"row": inward})

    def to_final(q):
        return remote(z_fin.at[q], z_in.at[q], z_fsem.at[0], zi_rsem.at[q], {"row": outward})

    def chunk_arrived(ch):
        for h in range(PARTS):
            for k in range(n_col - 1, 0, -1):
                for g in range(2):
                    ag_copy(ch, k, g, h, block_of(peer_from(k), g, h)).wait_recv()
            own_ag(ch, h, other, block_of(col, other, h)).wait_recv()

    def product(q):
        ch, p = lax.div(q, pieces), lax.rem(q, pieces)

        @pl.when((p == 0) & (ch > 0))
        def _():
            chunk_arrived(ch)

        left = jnp.concatenate([grads[ch, s] for s in range(2 * n_col * PARTS)], axis=1)
        at = pl.ds(pl.multiple_of(p * PIECE, PIECE), PIECE)
        if cached:
            right = dense[:, at]
        else:
            wide = PIECE // blk

            def gather(rb, carry):
                for i in range(wide):
                    tile = which(rb * col_blocks + p * wide + i)
                    strip[pl.ds(pl.multiple_of(rb * blk, blk), blk), i * blk:(i + 1) * blk] = tiles[tile]
                return carry

            lax.fori_loop(0, n_col * sub, gather, 0)
            right = strip[...]
        return jnp.dot(left, right, preferred_element_type=f32)

    def contribute(q):
        @pl.when(q < steps)
        def _():
            own_part[...] = product(q)

        if moved:
            @pl.when(q >= steps)
            def _():
                lend(0).wait_recv()
                own_part[...] = guest_in[0].astype(f32)

        part = own_part[...]

        @pl.when(has_outer)
        def _():
            to_sum(q).wait_recv()
            z_send[q] = (part + z_out[q].astype(f32)).astype(bf16)

        @pl.when(jnp.logical_not(has_outer))
        def _():
            z_send[q] = part.astype(bf16)

        @pl.when(is_mid)
        def _():
            to_cross(q).start()

        @pl.when(jnp.logical_not(is_mid))
        def _():
            to_sum(q).start()

    def finish(q):
        ch, p = lax.div(q, pieces), lax.rem(q, pieces)
        to_cross(q).wait_recv()

        @pl.when(is_mid)
        def _():
            z_fin[q] = (z_send[q].astype(f32) + z_in[q].astype(f32)).astype(bf16)

        @pl.when(jnp.logical_not(is_mid))
        def _():
            z_fin[q] = z_in[q]

        @pl.when(has_outer)
        def _():
            to_final(q).start()

        if moved:
            @pl.when(q >= steps)
            def _():
                give_back(HOSTS - col).start()

            @pl.when(home & (ch == CHUNKS - 1) & (p >= kept_here))
            def _():
                give_back(p - kept_here).wait_recv()

        @pl.when(ch == CHUNKS - 1)
        def _():
            whole = jnp.concatenate([z_fin[c * pieces + p] for c in range(CHUNKS)], axis=0)
            grad_input[pl.ds(pl.multiple_of(p * PIECE, PIECE), PIECE)] = jnp.transpose(whole)

    lag = LAG + depth * LAG_STEP
    longest = LAG + (n_row // 2 - 1) * LAG_STEP
    stages = (
        (weight_rows, 1, 3), (weight_cols, 5, 7), (weight_spread, 14, 18), (settle, 15, 19),
        (weight_done, steps + LAG, steps + longest - 5)
    )

    def z_step(j, carry):
        @pl.when(j < total)
        def _():
            contribute(piece_at(j))

        if moved:
            @pl.when(home & jnp.logical_not(has_outer) & (j < moved))
            def _():
                offer(j, 0)

        @pl.when((j >= lag) & (j < total + lag))
        def _():
            finish(piece_at(j - lag))

        for stage, inner, outer in stages:
            pl.when(j == jnp.where(has_outer, inner, outer))(stage)

        return carry

    def offer(m, carry):
        guest_send[m] = product(kept_here + m).astype(bf16)
        lend(m).start()
        return carry

    chunk_arrived(0)
    if moved:
        @pl.when(home & has_outer)
        def _():
            lax.fori_loop(0, moved, offer, 0)

    lax.fori_loop(0, steps + longest + (1 if moved else 0), z_step, 0)

    def all_sent(first, size):
        span = pl.ds(first, size)
        remote(z_send.at[span], z_out.at[span], z_ssem.at[0], zo_rsem.at[0], {"row": inward}).wait_send()

        @pl.when(has_outer)
        def _():
            remote(z_fin.at[span], z_in.at[span], z_fsem.at[0], zi_rsem.at[0], {"row": outward}).wait_send()

    if moved:
        @pl.when(home)
        def _():
            for m in range(moved):
                lend(m).wait_send()
            all_sent(0, steps - moved)

        @pl.when(guest)
        def _():
            give_back(HOSTS - col).wait_send()
            all_sent(0, steps + 1)

    @pl.when(jnp.logical_not(home | guest))
    def _():
        all_sent(0, steps)


def deliver(a_in, b_in, c_in, a_out, b_out, c_out, sems):
    pairs = ((a_in, a_out), (b_in, b_out), (c_in, c_out))
    stores = [pltpu.make_async_copy(src, dst, sems.at[i]) for i, (src, dst) in enumerate(pairs)]
    for copy in stores:
        copy.start()
    for copy in stores:
        copy.wait()


def per_device(
    tile_values, tile_rows, tile_cols, tile_mask, degree_caps, clip_groups,
    clip_bounds, features, weight, out_grad, dp_noise,
):
    tile_vals = tile_values[0, 0]
    slots, blk = tile_vals.shape[0], tile_vals.shape[1]
    node, half = out_grad.shape
    n_col, n_row = lax.axis_size("col"), lax.axis_size("row")
    col_range = features.shape[0]
    row_range = node * n_col
    hid = weight.shape[0]
    cached = row_range * col_range * 2 <= (20 << 20)
    pieces = col_range // PIECE
    places = -(-(row_range // blk) * (col_range // blk) // (8 * LANES)) * 8
    mine, nb, fc = node // 2, node // 2 // PARTS, half // CHUNKS
    wr, wrc = hid // n_row, hid // n_row // n_col
    steps = CHUNKS * pieces
    bf16, f32, i32 = jnp.bfloat16, jnp.float32, jnp.int32
    anywhere = pl.BlockSpec(memory_space=pl.ANY)
    sem, vmem, smem = pltpu.SemaphoreType.DMA, pltpu.VMEM, pltpu.SMEM
    shapes = (
        jax.ShapeDtypeStruct((node, half), bf16),
        jax.ShapeDtypeStruct((hid, half), f32),
        jax.ShapeDtypeStruct((col_range, half), bf16),
    )
    call = pl.pallas_call(
        functools.partial(layer, n_row, n_col, 1.0 / math.sqrt(node * n_col * n_row), cached),
        out_shape=tuple(pltpu.VMEM(x.shape, x.dtype) for x in shapes),
        in_specs=[anywhere] * 11,
        out_specs=[pl.BlockSpec(memory_space=pltpu.VMEM)] * 3,
        scratch_shapes=[
            smem((slots,), i32), smem((slots,), i32), smem((slots,), i32), smem(clip_bounds.shape, f32),
            smem((places, LANES), i32), vmem((places, LANES), i32),
            vmem((1, node), i32), vmem((1, node), i32),
            vmem((col_range, half), bf16),
            vmem((hid, hid), bf16),
            vmem((node, half), bf16),
            vmem((hid, half), f32),
            vmem((mine, half), bf16),
            vmem((slots + 1, blk, blk), bf16),
            vmem((row_range if cached else node, col_range), bf16),
            vmem((16, LANES) if cached else (row_range, PIECE), bf16),
            vmem((n_col - 1, 2, PARTS, nb, half), bf16),
            vmem((n_col - 1, 2, PARTS, nb, half), bf16),
            vmem((2, PARTS, nb, half), f32),
            vmem((2, PARTS, nb, half), f32),
            vmem((2, mine, half), bf16),
            vmem((mine, LANES), f32),
            vmem((mine, LANES), f32),
            vmem((2, mine, half), bf16),
            vmem((2, CHUNKS, PARTS, fc, nb), bf16),
            vmem((CHUNKS, 2 * n_col * PARTS, fc, nb), bf16),
            vmem((2, n_row, wr, half), bf16),
            vmem((n_row, 2, wr, half), bf16),
            vmem((n_col, wrc, half), f32),
            vmem((n_col, wrc, half), f32),
            vmem((n_row, wrc, half), f32),
            vmem((n_col, n_row, wrc, half), f32),
            vmem((fc, PIECE), f32),
            vmem((MOVED, fc, PIECE), bf16),
            vmem((1, fc, PIECE), bf16),
            vmem((steps + 1, fc, PIECE), bf16),
            vmem((steps + 1, fc, PIECE), bf16),
            vmem((steps + 1, fc, PIECE), bf16),
            vmem((steps + 1, fc, PIECE), bf16),
            sem((6,)), sem((1,)), sem((LOADS,)), sem((4,)), sem((2,)),
            sem((2, PARTS)), sem((2,)),
            sem((n_col - 1, 2, PARTS)), sem((n_col - 1, 2, PARTS)),
            sem((CHUNKS, n_col - 1, 2, PARTS)), sem((CHUNKS, 2 * n_col * PARTS)), sem((CHUNKS, PARTS)),
            sem((n_row, 2)), sem((n_row, 2)), sem((n_col - 1,)), sem((n_col,)),
            sem((n_row - 1,)), sem((n_row,)), sem((n_col - 1,)), sem((n_col,)),
            sem((1,)), sem((1,)), sem((steps + 1,)), sem((steps + 1,)),
            sem((MOVED,)), sem((1,)), sem((1,)), sem((MOVED,)),
        ],
        compiler_params=pltpu.CompilerParams(
            collective_id=0, has_side_effects=True, vmem_limit_bytes=56 << 20
        ),
        name="layer",
    )
    results = call(
        tile_vals, tile_rows[0, 0], tile_cols[0, 0], tile_mask[0, 0],
        degree_caps[None, :], clip_groups[None, :], clip_bounds,
        features, weight, out_grad, dp_noise,
    )
    return pl.pallas_call(
        deliver,
        out_shape=shapes,
        in_specs=[pl.BlockSpec(memory_space=pltpu.VMEM)] * 3,
        out_specs=[anywhere] * 3,
        scratch_shapes=[sem((3,))],
        compiler_params=pltpu.CompilerParams(vmem_limit_bytes=4 << 20),
        name="deliver",
    )(*results)


def solution(mesh):
    placed = (
        P("row", "col", None, None, None),
        P("row", "col", None),
        P("row", "col", None),
        P("row", "col", None),
        P(("row", "col")),
        P(("row", "col")),
        P(),
        P("col", "feat"),
        P(),
        P(("row", "col"), "feat"),
        P(None, "feat"),
    )
    return jax.shard_map(
        per_device,
        mesh=mesh,
        in_specs=placed,
        out_specs=(P(("row", "col"), "feat"), P(None, "feat"), P("col", "feat")),
        check_vma=False,
    )
```

```python
import functools
import math

import jax
import jax.numpy as jnp
from jax import lax
from jax.experimental import pallas as pl
from jax.experimental.pallas import tpu as pltpu
from jax.sharding import PartitionSpec as P

MESH = pl.DeviceIdType.MESH
LANES = 128
PIECE = 256
CHUNKS = 2
PARTS = 2
LOADS = 2
LAG = 4
LAG_STEP = 12
MOVED = 2
GUEST_AT = 7
HOSTS = 3


def layer(
    n_row, n_col, scale, cached,
    tiles_hbm, rows_hbm, cols_hbm, mask_hbm, caps_hbm, groups_hbm, bounds_hbm,
    feats_hbm, weight_hbm, og_hbm, noise_hbm,
    out_feat, grad_weight, grad_input,
    rows_s, cols_s, mask_s, bounds_s, map_s, map_v, caps, groups,
    feats, weight, out_grad, noise, feat_peer,
    tiles, dense, strip, rs_send, rs_recv, own_send, chip_part, cotangents,
    scale_col, bound_col, feat_halves, back_t, grads,
    w_send, w_recv, w_part, w_col, w_row, w_fin,
    own_part, guest_send, guest_in, z_send, z_out, z_in, z_fin,
    small_sem, map_sem, tile_sem, in_sem, og_sem, own_sem, of_sem,
    rs_ssem, rs_rsem, ag_ssem, ag_rsem, own_ag_sem,
    wz_ssem, wz_rsem, wc_ssem, wc_rsem, wr_ssem, wr_rsem, wf_ssem, wf_rsem,
    z_ssem, z_fsem, zo_rsem, zi_rsem, guest_ssem, guest_rsem, back_ssem, back_rsem,
):
    row, col, feat = lax.axis_index("row"), lax.axis_index("col"), lax.axis_index("feat")
    other = 1 - feat
    f32, bf16 = jnp.float32, jnp.bfloat16
    slots, blk = tiles_hbm.shape[0], tiles_hbm.shape[1]
    node, half = og_hbm.shape
    col_range = feats.shape[0]
    col_blocks = col_range // blk
    sub = node // blk
    mine = node // 2
    nb = mine // PARTS
    hid = weight.shape[0]
    fc = half // CHUNKS
    pieces = col_range // PIECE
    side = math.isqrt(n_col)
    side = side if side * side == n_col else n_col
    col_x, col_y = lax.rem(col, side), lax.div(col, side)
    wr = hid // n_row
    wrc = wr // n_col

    def remote(src, dst, ssem, rsem, where):
        return pltpu.make_async_remote_copy(
            src_ref=src, dst_ref=dst, send_sem=ssem, recv_sem=rsem,
            device_id=where, device_id_type=MESH,
        )

    def peer_to(k):
        x, y = k % side, k // side
        return lax.rem(col_y + y, n_col // side) * side + lax.rem(col_x + x, side)

    def peer_from(k):
        x, y = k % side, k // side
        up = n_col // side
        return lax.rem(col_y - y + up, up) * side + lax.rem(col_x - x + side, side)

    small = [
        pltpu.make_async_copy(src, dst, small_sem.at[i])
        for i, (src, dst) in enumerate((
            (rows_hbm, rows_s), (cols_hbm, cols_s), (mask_hbm, mask_s), (bounds_hbm, bounds_s),
            (caps_hbm, caps), (groups_hbm, groups),
        ))
    ]
    count = slots // LOADS
    loads = [
        pltpu.make_async_copy(
            tiles_hbm.at[pl.ds(i * count, count)], tiles.at[pl.ds(i * count, count)], tile_sem.at[i]
        )
        for i in range(LOADS)
    ]
    inputs = [
        pltpu.make_async_copy(src, dst, in_sem.at[i])
        for i, (src, dst) in enumerate(
            ((feats_hbm, feats), (og_hbm, out_grad), (weight_hbm, weight), (noise_hbm, noise))
        )
    ]
    for copy in loads + inputs[:1] + small:
        copy.start()

    barrier = pltpu.get_barrier_semaphore()

    def greet(where):
        pl.semaphore_signal(barrier, inc=1, device_id=where, device_id_type=MESH)

    greet({"feat": other})
    for g in range(2):
        for k in range(1, n_col):
            greet({"col": peer_to(k), "feat": g})
        for step in range(1, n_row):
            greet({"row": lax.rem(row + step, n_row), "feat": g})

    for copy in inputs[1:]:
        copy.start()
    tiles[slots] = jnp.zeros((blk, blk), bf16)
    for copy in small[:3]:
        copy.wait()
    spot = lax.broadcasted_iota(jnp.int32, map_v.shape, 0) * LANES + lax.broadcasted_iota(jnp.int32, map_v.shape, 1)

    def place(k, found):
        at = jnp.where(mask_s[k] == 1, rows_s[k] * col_blocks + cols_s[k], -1)
        return jnp.where(spot == at, k, found)

    map_v[...] = lax.fori_loop(0, slots, place, jnp.full(map_v.shape, slots, jnp.int32), unroll=8)
    map_copy = pltpu.make_async_copy(map_v, map_s, map_sem.at[0])
    map_copy.start()
    for copy in small[3:]:
        copy.wait()

    def column(values):
        return jnp.transpose(jnp.broadcast_to(values, (LANES, mine)))

    my_nodes = pl.ds(pl.multiple_of(feat * mine, mine), mine)
    scale_row = lax.rsqrt(caps[:, my_nodes].astype(f32))
    scale_col[...] = column(scale_row)
    bound = jnp.zeros((1, mine), f32)
    for g in range(bounds_s.shape[0]):
        bound = bound + jnp.where(groups[:, my_nodes] == g, bounds_s[g], 0.0)
    bound_col[...] = column(bound)
    map_copy.wait()
    inputs[0].wait()
    for copy in loads:
        copy.wait()

    def which(index):
        return map_s[index // LANES, index % LANES] if isinstance(index, int) else map_s[lax.div(index, LANES), lax.rem(index, LANES)]

    def assemble(chunk, h, groups_of):
        base = chunk * node if cached else 0
        for g in groups_of:
            for b in range(nb // blk):
                rb = (g * mine + h * nb) // blk + b
                at = pl.ds(pl.multiple_of(base + rb * blk, blk), blk)
                for cb in range(col_blocks):
                    tile = which((chunk * sub + rb) * col_blocks + cb)
                    dense[at, cb * blk:(cb + 1) * blk] = tiles[tile]

    def partial_sum(chunk, h, groups_of=(0, 1)):
        assemble(chunk, h, groups_of)
        base = chunk * node if cached else 0
        left = jnp.concatenate(
            [dense[pl.ds(pl.multiple_of(base + g * mine + h * nb, blk), nb), :] for g in groups_of], axis=0
        )
        return jnp.dot(left, feats[...], preferred_element_type=f32)

    def rs_copy(k, h, g, sender):
        return remote(
            rs_send.at[k - 1, g, h], rs_recv.at[k - 1, sender, h],
            rs_ssem.at[k - 1, g, h], rs_rsem.at[k - 1, sender, h],
            {"col": peer_to(k), "feat": g},
        )

    def make(k, h):
        part = partial_sum(peer_to(k), h).astype(bf16)
        for g in range(2):
            rs_send[k - 1, g, h] = part[g * nb:(g + 1) * nb]

    def push(k, h):
        for g in range(2):
            rs_copy(k, h, g, feat).start()

    def own_copy(h, sender):
        return remote(
            own_send.at[1 - sender, h], chip_part.at[sender, h],
            own_sem.at[0, h], own_sem.at[1, h], {"feat": other},
        )

    def make_own(h):
        part = partial_sum(col, h)
        for g in range(2):
            own_send[g, h] = part[g * nb:(g + 1) * nb]
        own_copy(h, feat).start()
        chip_part[feat, h] = own_send[feat, h]

    for g in range(2):
        rs_send[n_col - 2, g, 0] = partial_sum(peer_to(n_col - 1), 0, (g,)).astype(bf16)
        if g == 0:
            pl.semaphore_wait(barrier, 2 * (n_col + n_row) - 3)
        rs_copy(n_col - 1, 0, g, feat).start()
    for copy in inputs[1:]:
        copy.wait()
    theirs = pl.ds(pl.multiple_of(other * mine, mine), mine)
    og_copy = remote(out_grad.at[theirs], cotangents.at[feat], og_sem.at[0], og_sem.at[1], {"feat": other})
    og_copy.start()

    for h in range(PARTS):
        def forward(i, carry):
            k = n_col - 1 - i
            make(k, h)
            push(k, h)
            return carry

        lax.fori_loop(1 if h == 0 else 0, n_col - 1, forward, 0)
        make_own(h)

    def block_of(c, g, h):
        return (c * 2 + g) * PARTS + h

    def ag_copy(ch, k, g, h, sender):
        return remote(
            back_t.at[g, ch, h], grads.at[ch, sender],
            ag_ssem.at[ch, k - 1, g, h], ag_rsem.at[ch, sender], {"col": peer_to(k), "feat": g},
        )

    def own_ag(ch, h, g, sender):
        return remote(
            back_t.at[g, ch, h], grads.at[ch, sender],
            own_ag_sem.at[ch, h], ag_rsem.at[ch, sender], {"feat": other},
        )

    w_total = jnp.zeros((hid, hid), f32)
    remote(out_grad.at[theirs], cotangents.at[other], og_sem.at[0], og_sem.at[1], {"feat": other}).wait_recv()
    cotangents[feat] = out_grad[pl.ds(pl.multiple_of(feat * mine, mine), mine)]
    for h in range(PARTS):
        spot_h = slice(h * nb, (h + 1) * nb)
        own_copy(h, other).wait_recv()
        sums = [chip_part[0, h], chip_part[1, h]]
        for k in range(n_col - 1, 0, -1):
            for g in range(2):
                rs_copy(k, h, g, g).wait_recv()
                sums[g] = sums[g] + rs_recv[k - 1, g, h].astype(f32)
        node_scale = scale_col[spot_h]
        agg = jnp.concatenate([(s * node_scale).astype(bf16) for s in sums], axis=1)
        cotangent = jnp.concatenate([cotangents[0, spot_h], cotangents[1, spot_h]], axis=1)
        pre = jnp.dot(agg, weight[...], preferred_element_type=f32)
        sig = 1.0 / (1.0 + jnp.exp(-pre))
        grad = (cotangent.astype(f32) * sig * (1.0 + pre * (1.0 - sig))).astype(bf16)
        me = block_of(col, feat, h)
        for ch in range(CHUNKS):
            rows = jnp.concatenate([weight[g * half + ch * fc:g * half + (ch + 1) * fc] for g in range(2)], axis=0)
            back = lax.dot_general(rows, grad, (((1,), (1,)), ((), ())), preferred_element_type=f32)
            back = (back * scale_row[:, spot_h]).astype(bf16)
            for g in range(2):
                back_t[g, ch, h] = back[g * fc:(g + 1) * fc]
            for k in range(n_col - 1, 0, -1):
                for g in range(2):
                    ag_copy(ch, k, g, h, me).start()
            own_ag(ch, h, other, me).start()
            grads[ch, me] = back_t[feat, ch, h]
        activated = (pre * sig).astype(bf16)
        for g in range(2):
            feat_halves[g, h * nb:(h + 1) * nb] = activated[:, g * half:(g + 1) * half]

        def norm(value):
            value = value.astype(f32)
            return jnp.sqrt(jnp.sum(value * value, axis=1, keepdims=True) + 1e-06)

        factor = jnp.minimum(1.0, bound_col[spot_h] / (norm(agg) * norm(grad)))
        wide = grad.astype(f32)
        clipped = jnp.concatenate(
            [(factor * wide[:, g * half:(g + 1) * half]).astype(bf16) for g in range(2)], axis=1
        )
        w_total = w_total + lax.dot_general(agg, clipped, (((0,), (0,)), ((), ())), preferred_element_type=f32)

    def wz_copy(step, g, r, s):
        return remote(
            w_send.at[g, lax.rem(row + step, n_row)], w_recv.at[r, s],
            wz_ssem.at[step, g], wz_rsem.at[r, s], {"row": lax.rem(row + step, n_row), "feat": g},
        )

    def wz_own(r, s):
        return remote(
            w_send.at[other, row], w_recv.at[r, s], wz_ssem.at[0, 0], wz_rsem.at[r, s], {"feat": other}
        )

    for g in range(2):
        for r in range(n_row):
            w_send[g, r] = w_total[r * wr:(r + 1) * wr, g * half:(g + 1) * half].astype(bf16)
    w_recv[row, feat] = w_send[feat, row]
    for step in range(1, n_row):
        for g in range(2):
            wz_copy(step, g, row, feat).start()
    wz_own(row, feat).start()

    of_copy = remote(feat_halves.at[other], feat_peer, of_sem.at[0], of_sem.at[1], {"feat": other})
    of_copy.start()
    kept = pl.ds(pl.multiple_of(feat * mine, mine), mine)
    out_feat[kept] = feat_halves[feat]

    def wc_copy(k, sender):
        return remote(
            w_part.at[peer_to(k)], w_col.at[sender], wc_ssem.at[k - 1], wc_rsem.at[sender], {"col": peer_to(k)}
        )

    def wr_copy(step, sender):
        spot = w_row.at[sender]
        return remote(spot, spot, wr_ssem.at[step - 1], wr_rsem.at[sender], {"row": lax.rem(row + step, n_row)})

    def wf_copy(k, sender):
        spot = w_fin.at[sender]
        return remote(spot, spot, wf_ssem.at[k - 1], wf_rsem.at[sender], {"col": peer_to(k)})

    def weight_rows():
        for step in range(1, n_row):
            for g in range(2):
                wz_copy(step, g, lax.rem(row - step + n_row, n_row), g).wait_recv()
        wz_own(row, other).wait_recv()
        total = jnp.zeros((wr, half), f32)
        for r in range(n_row):
            for g in range(2):
                total = total + w_recv[r, g].astype(f32)
        for c in range(n_col):
            w_part[c] = total[c * wrc:(c + 1) * wrc]
        for k in range(1, n_col):
            wc_copy(k, col).start()
        w_col[col] = w_part[col]

    def weight_cols():
        for k in range(1, n_col):
            wc_copy(k, peer_from(k)).wait_recv()
        total = w_col[0]
        for c in range(1, n_col):
            total = total + w_col[c]
        w_row[row] = total
        for step in range(1, n_row):
            wr_copy(step, row).start()

    def weight_spread():
        for step in range(1, n_row):
            wr_copy(step, lax.rem(row - step + n_row, n_row)).wait_recv()
        w_fin[col] = w_row[...]
        for k in range(1, n_col):
            wf_copy(k, col).start()

    def settle():
        of_copy.wait()
        out_feat[theirs] = feat_peer[...]
        og_copy.wait_send()
        for h in range(PARTS):
            own_copy(h, feat).wait_send()
            for ch in range(CHUNKS):
                own_ag(ch, h, other, block_of(col, feat, h)).wait_send()
            for k in range(1, n_col):
                for g in range(2):
                    rs_copy(k, h, g, feat).wait_send()
                    for ch in range(CHUNKS):
                        ag_copy(ch, k, g, h, block_of(col, feat, h)).wait_send()
        for step in range(1, n_row):
            for g in range(2):
                wz_copy(step, g, row, feat).wait_send()
        wz_own(row, feat).wait_send()

    def weight_done():
        for k in range(1, n_col):
            wf_copy(k, peer_from(k)).wait_recv()
        for c in range(n_col):
            for r in range(n_row):
                at = r * wr + c * wrc
                grad_weight[at:at + wrc] = w_fin[c, r] * scale + noise[at:at + wrc]
        for step in range(1, n_row):
            wr_copy(step, row).wait_send()
        for k in range(1, n_col):
            wc_copy(k, col).wait_send()
            wf_copy(k, col).wait_send()

    last = n_row - 1
    lower = row < n_row // 2
    inward = jnp.where(lower, row + 1, row - 1)
    outward = jnp.where(lower, row - 1, row + 1)
    depth = jnp.where(lower, n_row // 2 - 1 - row, row - n_row // 2)
    is_mid = depth == 0
    has_outer = (row > 0) & (row < last)
    steps = CHUNKS * pieces
    moved = MOVED if n_col > HOSTS else 0
    kept_here = pieces - moved
    home = col == 0 if moved else col < 0
    guest = (col == HOSTS) | (col == HOSTS - 2)
    total = jnp.where(home, steps - moved, jnp.where(guest, steps + 1, steps))

    def piece_at(j):
        late = jnp.where(j == GUEST_AT, steps, j - 1)
        own = jnp.where(j < kept_here, j, j + moved)
        return jnp.where(home, own, jnp.where(guest & (j >= GUEST_AT), late, j))

    def lend(m):
        return remote(
            guest_send.at[m], guest_in.at[0], guest_ssem.at[m], guest_rsem.at[0], {"col": HOSTS - 2 * m}
        )

    def give_back(m):
        return remote(z_fin.at[steps], z_fin.at[kept_here + m], back_ssem.at[0], back_rsem.at[m], {"col": 0})

    def to_sum(q):
        return remote(z_send.at[q], z_out.at[q], z_ssem.at[0], zo_rsem.at[q], {"row": inward})

    def to_cross(q):
        return remote(z_send.at[q], z_in.at[q], z_ssem.at[0], zi_rsem.at[q], {"row": inward})

    def to_final(q):
        return remote(z_fin.at[q], z_in.at[q], z_fsem.at[0], zi_rsem.at[q], {"row": outward})

    def chunk_arrived(ch):
        for h in range(PARTS):
            for k in range(n_col - 1, 0, -1):
                for g in range(2):
                    ag_copy(ch, k, g, h, block_of(peer_from(k), g, h)).wait_recv()
            own_ag(ch, h, other, block_of(col, other, h)).wait_recv()

    def product(q):
        ch, p = lax.div(q, pieces), lax.rem(q, pieces)

        @pl.when((p == 0) & (ch > 0))
        def _():
            chunk_arrived(ch)

        left = jnp.concatenate([grads[ch, s] for s in range(2 * n_col * PARTS)], axis=1)
        at = pl.ds(pl.multiple_of(p * PIECE, PIECE), PIECE)
        if cached:
            right = dense[:, at]
        else:
            wide = PIECE // blk

            def gather(rb, carry):
                for i in range(wide):
                    tile = which(rb * col_blocks + p * wide + i)
                    strip[pl.ds(pl.multiple_of(rb * blk, blk), blk), i * blk:(i + 1) * blk] = tiles[tile]
                return carry

            lax.fori_loop(0, n_col * sub, gather, 0)
            right = strip[...]
        return jnp.dot(left, right, preferred_element_type=f32)

    def contribute(q):
        @pl.when(q < steps)
        def _():
            own_part[...] = product(q)

        if moved:
            @pl.when(q >= steps)
            def _():
                lend(0).wait_recv()
                own_part[...] = guest_in[0].astype(f32)

        part = own_part[...]

        @pl.when(has_outer)
        def _():
            to_sum(q).wait_recv()
            z_send[q] = (part + z_out[q].astype(f32)).astype(bf16)

        @pl.when(jnp.logical_not(has_outer))
        def _():
            z_send[q] = part.astype(bf16)

        @pl.when(is_mid)
        def _():
            to_cross(q).start()

        @pl.when(jnp.logical_not(is_mid))
        def _():
            to_sum(q).start()

    def finish(q):
        ch, p = lax.div(q, pieces), lax.rem(q, pieces)
        to_cross(q).wait_recv()

        @pl.when(is_mid)
        def _():
            z_fin[q] = (z_send[q].astype(f32) + z_in[q].astype(f32)).astype(bf16)

        @pl.when(jnp.logical_not(is_mid))
        def _():
            z_fin[q] = z_in[q]

        @pl.when(has_outer)
        def _():
            to_final(q).start()

        if moved:
            @pl.when(q >= steps)
            def _():
                give_back((HOSTS - col) // 2).start()

            @pl.when(home & (ch == CHUNKS - 1) & (p >= kept_here))
            def _():
                give_back(p - kept_here).wait_recv()

        @pl.when(ch == CHUNKS - 1)
        def _():
            whole = jnp.concatenate([z_fin[c * pieces + p] for c in range(CHUNKS)], axis=0)
            grad_input[pl.ds(pl.multiple_of(p * PIECE, PIECE), PIECE)] = jnp.transpose(whole)

    lag = LAG + depth * LAG_STEP
    longest = LAG + (n_row // 2 - 1) * LAG_STEP
    stages = (
        (weight_rows, 1, 3), (weight_cols, 5, 7), (weight_spread, 14, 18), (settle, 15, 19),
        (weight_done, steps + LAG, steps + longest - 5)
    )

    def z_step(j, carry):
        @pl.when(j < total)
        def _():
            contribute(piece_at(j))

        if moved:
            @pl.when(home & jnp.logical_not(has_outer) & (j < moved))
            def _():
                offer(j, 0)

        @pl.when((j >= lag) & (j < total + lag))
        def _():
            finish(piece_at(j - lag))

        for stage, inner, outer in stages:
            pl.when(j == jnp.where(has_outer, inner, outer))(stage)

        return carry

    def offer(m, carry):
        guest_send[m] = product(kept_here + m).astype(bf16)
        lend(m).start()
        return carry

    chunk_arrived(0)
    if moved:
        @pl.when(home & has_outer)
        def _():
            lax.fori_loop(0, moved, offer, 0)

    lax.fori_loop(0, steps + longest + (1 if moved else 0), z_step, 0)

    def all_sent(first, size):
        span = pl.ds(first, size)
        remote(z_send.at[span], z_out.at[span], z_ssem.at[0], zo_rsem.at[0], {"row": inward}).wait_send()

        @pl.when(has_outer)
        def _():
            remote(z_fin.at[span], z_in.at[span], z_fsem.at[0], zi_rsem.at[0], {"row": outward}).wait_send()

    if moved:
        @pl.when(home)
        def _():
            for m in range(moved):
                lend(m).wait_send()
            all_sent(0, steps - moved)

        @pl.when(guest)
        def _():
            give_back((HOSTS - col) // 2).wait_send()
            all_sent(0, steps + 1)

    @pl.when(jnp.logical_not(home | guest))
    def _():
        all_sent(0, steps)


def deliver(a_in, b_in, c_in, a_out, b_out, c_out, sems):
    pairs = ((a_in, a_out), (b_in, b_out), (c_in, c_out))
    stores = [pltpu.make_async_copy(src, dst, sems.at[i]) for i, (src, dst) in enumerate(pairs)]
    for copy in stores:
        copy.start()
    for copy in stores:
        copy.wait()


def per_device(
    tile_values, tile_rows, tile_cols, tile_mask, degree_caps, clip_groups,
    clip_bounds, features, weight, out_grad, dp_noise,
):
    tile_vals = tile_values[0, 0]
    slots, blk = tile_vals.shape[0], tile_vals.shape[1]
    node, half = out_grad.shape
    n_col, n_row = lax.axis_size("col"), lax.axis_size("row")
    col_range = features.shape[0]
    row_range = node * n_col
    hid = weight.shape[0]
    cached = row_range * col_range * 2 <= (20 << 20)
    pieces = col_range // PIECE
    places = -(-(row_range // blk) * (col_range // blk) // (8 * LANES)) * 8
    mine, nb, fc = node // 2, node // 2 // PARTS, half // CHUNKS
    wr, wrc = hid // n_row, hid // n_row // n_col
    steps = CHUNKS * pieces
    bf16, f32, i32 = jnp.bfloat16, jnp.float32, jnp.int32
    anywhere = pl.BlockSpec(memory_space=pl.ANY)
    sem, vmem, smem = pltpu.SemaphoreType.DMA, pltpu.VMEM, pltpu.SMEM
    shapes = (
        jax.ShapeDtypeStruct((node, half), bf16),
        jax.ShapeDtypeStruct((hid, half), f32),
        jax.ShapeDtypeStruct((col_range, half), bf16),
    )
    call = pl.pallas_call(
        functools.partial(layer, n_row, n_col, 1.0 / math.sqrt(node * n_col * n_row), cached),
        out_shape=tuple(pltpu.VMEM(x.shape, x.dtype) for x in shapes),
        in_specs=[anywhere] * 11,
        out_specs=[pl.BlockSpec(memory_space=pltpu.VMEM)] * 3,
        scratch_shapes=[
            smem((slots,), i32), smem((slots,), i32), smem((slots,), i32), smem(clip_bounds.shape, f32),
            smem((places, LANES), i32), vmem((places, LANES), i32),
            vmem((1, node), i32), vmem((1, node), i32),
            vmem((col_range, half), bf16),
            vmem((hid, hid), bf16),
            vmem((node, half), bf16),
            vmem((hid, half), f32),
            vmem((mine, half), bf16),
            vmem((slots + 1, blk, blk), bf16),
            vmem((row_range if cached else node, col_range), bf16),
            vmem((16, LANES) if cached else (row_range, PIECE), bf16),
            vmem((n_col - 1, 2, PARTS, nb, half), bf16),
            vmem((n_col - 1, 2, PARTS, nb, half), bf16),
            vmem((2, PARTS, nb, half), f32),
            vmem((2, PARTS, nb, half), f32),
            vmem((2, mine, half), bf16),
            vmem((mine, LANES), f32),
            vmem((mine, LANES), f32),
            vmem((2, mine, half), bf16),
            vmem((2, CHUNKS, PARTS, fc, nb), bf16),
            vmem((CHUNKS, 2 * n_col * PARTS, fc, nb), bf16),
            vmem((2, n_row, wr, half), bf16),
            vmem((n_row, 2, wr, half), bf16),
            vmem((n_col, wrc, half), f32),
            vmem((n_col, wrc, half), f32),
            vmem((n_row, wrc, half), f32),
            vmem((n_col, n_row, wrc, half), f32),
            vmem((fc, PIECE), f32),
            vmem((MOVED, fc, PIECE), bf16),
            vmem((1, fc, PIECE), bf16),
            vmem((steps + 1, fc, PIECE), bf16),
            vmem((steps + 1, fc, PIECE), bf16),
            vmem((steps + 1, fc, PIECE), bf16),
            vmem((steps + 1, fc, PIECE), bf16),
            sem((6,)), sem((1,)), sem((LOADS,)), sem((4,)), sem((2,)),
            sem((2, PARTS)), sem((2,)),
            sem((n_col - 1, 2, PARTS)), sem((n_col - 1, 2, PARTS)),
            sem((CHUNKS, n_col - 1, 2, PARTS)), sem((CHUNKS, 2 * n_col * PARTS)), sem((CHUNKS, PARTS)),
            sem((n_row, 2)), sem((n_row, 2)), sem((n_col - 1,)), sem((n_col,)),
            sem((n_row - 1,)), sem((n_row,)), sem((n_col - 1,)), sem((n_col,)),
            sem((1,)), sem((1,)), sem((steps + 1,)), sem((steps + 1,)),
            sem((MOVED,)), sem((1,)), sem((1,)), sem((MOVED,)),
        ],
        compiler_params=pltpu.CompilerParams(
            collective_id=0, has_side_effects=True, vmem_limit_bytes=56 << 20
        ),
        name="layer",
    )
    results = call(
        tile_vals, tile_rows[0, 0], tile_cols[0, 0], tile_mask[0, 0],
        degree_caps[None, :], clip_groups[None, :], clip_bounds,
        features, weight, out_grad, dp_noise,
    )
    return pl.pallas_call(
        deliver,
        out_shape=shapes,
        in_specs=[pl.BlockSpec(memory_space=pltpu.VMEM)] * 3,
        out_specs=[anywhere] * 3,
        scratch_shapes=[sem((3,))],
        compiler_params=pltpu.CompilerParams(vmem_limit_bytes=4 << 20),
        name="deliver",
    )(*results)


def solution(mesh):
    placed = (
        P("row", "col", None, None, None),
        P("row", "col", None),
        P("row", "col", None),
        P("row", "col", None),
        P(("row", "col")),
        P(("row", "col")),
        P(),
        P("col", "feat"),
        P(),
        P(("row", "col"), "feat"),
        P(None, "feat"),
    )
    return jax.shard_map(
        per_device,
        mesh=mesh,
        in_specs=placed,
        out_specs=(P(("row", "col"), "feat"), P(None, "feat"), P("col", "feat")),
        check_vma=False,
    )
```
